32 devices in a mesh: sub: 8 (over z, x), blk: 4 (over y, core).
Axes of the slice: x: 2, y: 2, z: 4, core: 2. Of those that a mesh axis runs over, the one named last changes fastest.
Arguments:
- coefficients: float32 [512, 4, 2, 64, 128], P('sub', None, None, 'blk'), may hold values from -0.2 to 0.2
- owner_slot: int32 [512], P('sub'), may hold values from 0 to 511, as said below
- child_list: int32 [512, 8], P('sub'), may hold values from 0 to 7, each once within a row
Outputs:
- children: float32 [512, 4, 8, 64, 2, 128], P('sub', None, None, 'blk')
The draws below stay inside these ranges and needn't reach their ends.
Inputs may be any that keep to these rules, and one draw needn't show every extreme that they name: owner_slot is a permutation of the 512 positions; position s belongs to subtree index s // 64; of the 64 boxes held by one subtree index exactly 8 belong to each subtree index. `child_list`: each row lists the 8 octant codes once each.
All inputs are finite; a program needn't handle non-finite values.
Results may differ from the reference program's by a relative error of at most 0.0003.
Values sent between devices are 32-bit elements; how exact they have to be, the bound alone decides.
A program may use at most 128 MiB of HBM per device.

```python
import jax
import jax.numpy as jnp
from jax import lax

L = 64
M = 128
J = 64
K = 128
BOX_DEV = 64
NRHS = 4
BOXES = 512


def draw_owner_slot(key, part):
    sub_count = BOXES // BOX_DEV
    per_peer = BOX_DEV // sub_count
    first_key, second_key = jax.random.split(jax.random.fold_in(key, 11), 2)
    local_order = jax.vmap(lambda one: jax.random.permutation(one, BOX_DEV))(jax.random.split(first_key, sub_count))
    inside = jax.vmap(lambda one: jax.random.permutation(one, BOX_DEV))(jax.random.split(second_key, sub_count))
    ranks = jnp.arange(BOX_DEV, dtype=jnp.int32)
    target = ranks // per_peer
    within = ranks % per_peer
    sources = jnp.arange(sub_count, dtype=jnp.int32)[:, None]
    positions = inside[target[None, :], sources * per_peer + within[None, :]]
    slot_by_rank = target[None, :] * BOX_DEV + positions
    inverse = jnp.argsort(local_order, axis=1)
    slots = jnp.take_along_axis(slot_by_rank, inverse, axis=1)
    return slots.reshape(BOXES).astype(jnp.int32)


def steps_of(own_key, shape, cuts, least, largest):
    loudness, own = 1.0, jax.random.fold_in(own_key, 6)
    for position, blocks in cuts:
        heights = jnp.exp(jax.random.uniform(jax.random.fold_in(own, position), (blocks,), jnp.float32, least / len(cuts), largest / len(cuts)))
        loudness = loudness * jnp.repeat(heights, shape[position] // blocks).reshape([-1 if axis == position else 1 for axis in range(len(shape))])
    return loudness


def centred(rng, extent, width, reach, cuts=(), kind=jnp.bfloat16):
    entries = width * jax.random.normal(rng, extent, jnp.float32)
    if cuts:
        entries = entries * steps_of(rng, extent, cuts, -0.22, 0.18)
    return jnp.clip(entries, -reach, reach).astype(kind)


def setup_inputs(seed: int = 0) -> dict:
    key_of = jax.random.split(jax.random.key(seed), 4)
    coefficients = centred(key_of[0], (BOXES, NRHS, 2, L, M), 0.03, 0.2, ((0, 8), (3, 4)), jnp.float32)
    owner_slot = draw_owner_slot(jax.random.fold_in(key_of[3], 71), 0)
    child_list = jax.vmap(lambda own: jax.random.permutation(own, 8))(jax.random.split(key_of[2], BOXES)).reshape((BOXES, 8)).astype(jnp.int32)
    return {"coefficients": coefficients, "owner_slot": owner_slot, "child_list": child_list}


def legendre_table(orders_abs, polar, degrees):
    cosines = jnp.cos(polar)[None, :]
    sines = jnp.sin(polar)[None, :]
    order_col = orders_abs[:, None]
    log_start = 0.5 * (jnp.log((2.0 * order_col + 1.0) / (4.0 * jnp.pi)) + lax.lgamma(2.0 * order_col + 1.0) - order_col * jnp.log(4.0) - 2.0 * lax.lgamma(order_col + 1.0)) + order_col * jnp.log(sines)
    diag_value = jnp.exp(log_start)
    next_value = jnp.sqrt(2.0 * order_col + 3.0) * cosines * diag_value

    def advance(state, degree):
        previous, before, factor_prev = state
        numer = jnp.maximum(4.0 * degree * degree - 1.0, 1.0)
        denom = jnp.maximum(degree * degree - order_col * order_col, 1.0)
        factor = jnp.sqrt(numer / denom)
        recur = factor * (cosines * previous - before / factor_prev)
        value = jnp.where(degree < order_col, 0.0, jnp.where(degree == order_col, diag_value, jnp.where(degree == order_col + 1.0, next_value, recur)))
        return ((value, previous, factor), value)
    zeros = jnp.zeros_like(diag_value)
    start_state = (zeros, zeros, jnp.ones_like(order_col))
    _, values = lax.scan(advance, start_state, jnp.arange(degrees).astype(jnp.float32))
    return values

def dft_table(degrees, columns, azimuths):
    column_ids = jnp.arange(columns, dtype=jnp.int32)
    azimuth_ids = jnp.arange(azimuths, dtype=jnp.int32)
    turns = jnp.mod((column_ids[:, None] - degrees) * azimuth_ids[None, :], azimuths)
    angle = 2.0 * jnp.pi * turns.astype(jnp.float32) / azimuths
    cosine = jnp.cos(angle)
    sine = jnp.sin(angle)
    upper = jnp.concatenate([cosine, sine], axis=1)
    lower = jnp.concatenate([-sine, cosine], axis=1)
    return jnp.concatenate([upper, lower], axis=0)

def shift_children(waves, octants, polar, azimuths):
    azimuth = 2.0 * jnp.pi * jnp.arange(azimuths).astype(jnp.float32) / azimuths
    dir_x = jnp.sin(polar)[:, None] * jnp.cos(azimuth)[None, :]
    dir_y = jnp.sin(polar)[:, None] * jnp.sin(azimuth)[None, :]
    dir_z = jnp.cos(polar)[:, None] * jnp.ones_like(azimuth)[None, :]
    sign_x = (2 * (octants & 1) - 1).astype(jnp.float32)[:, None, None]
    sign_y = (2 * (octants >> 1 & 1) - 1).astype(jnp.float32)[:, None, None]
    sign_z = (2 * (octants >> 2 & 1) - 1).astype(jnp.float32)[:, None, None]
    phase = 5.5 * (sign_x * dir_x[None] + sign_y * dir_y[None] + sign_z * dir_z[None])
    phase_cos = jnp.cos(phase)[None]
    phase_sin = jnp.sin(phase)[None]
    wave_re = waves[:, :, 0, :][:, None]
    wave_im = waves[:, :, 1, :][:, None]
    real_part = wave_re * phase_cos - wave_im * phase_sin
    imag_part = wave_re * phase_sin + wave_im * phase_cos
    return jnp.stack([real_part, imag_part], axis=-2)

def reference(coefficients, owner_slot, child_list):
    owned = coefficients[jnp.argsort(owner_slot)]
    polar = jnp.pi * (jnp.arange(J).astype(jnp.float32) + 0.5) / J
    orders_abs = jnp.abs(jnp.arange(M) - L).astype(jnp.float32)
    table = legendre_table(orders_abs, polar, L)
    spectral = dft_table(L, M, K)
    cases = coefficients.shape[1]

    def one_box(inputs):
        expansion, octants = inputs
        cycles = jnp.einsum('rxlc,lcj->rjxc', expansion, table, precision=lax.Precision.HIGHEST)
        waves = jnp.dot(cycles.reshape(cases * J, 2 * M), spectral, precision=lax.Precision.HIGHEST)
        return shift_children(waves.reshape(cases, J, 2, K), octants, polar, K)
    return lax.map(one_box, (owned, child_list))
```

```python
import functools
import math

import jax
import jax.numpy as jnp
import numpy as np
from jax import lax
from jax.experimental import pallas as pl
from jax.experimental.pallas import tpu as pltpu
from jax.sharding import PartitionSpec as P

J = 64
K = 128
LANES = 128
MIB = 1024 * 1024


def ceil_div(value, by):
    return (value + by - 1) // by


def packed_rows(depth, part):
    return ceil_div(depth * depth * (2 * part + 1), LANES)


def first_lane(depth, part, inner):
    return inner * (2 * depth * part) + inner * inner


def swapped(index, step, size):
    total = 0
    bit = 1
    while bit < size:
        total = total + ((index // bit + step // bit) % 2) * bit
        bit *= 2
    return total


def legendre_constants(degrees, columns, parts):
    order = np.abs(np.arange(columns) - degrees).astype(np.float64)
    log_norm = np.array(
        [
            0.5
            * (
                math.log((2 * v + 1) / (4 * math.pi))
                + math.lgamma(2 * v + 1)
                - v * math.log(4.0)
                - 2 * math.lgamma(v + 1)
            )
            for v in order
        ]
    )
    polar = np.pi * (np.arange(J) + 0.5) / J
    diag = np.exp(log_norm[None] + order[None] * np.log(np.sin(polar))[:, None])
    cosines = np.broadcast_to(np.cos(polar)[:, None], (J, columns))
    level = np.arange(degrees, dtype=np.float64)[:, None]
    factor = np.sqrt(np.maximum(4 * level * level - 1, 1.0) / np.maximum(level * level - order[None] ** 2, 1.0))
    before = np.ones_like(factor)
    before[1:] = 1.0 / factor[:-1]
    shape = (parts, J // parts, columns)
    return (
        diag.astype(np.float32).reshape(shape),
        cosines.astype(np.float32).reshape(shape),
        order.astype(np.float32)[None],
        factor.astype(np.float32)[:, None, :],
        before.astype(np.float32)[:, None, :],
    )


def wave_matrix(degrees, columns, azimuths):
    turns = ((np.arange(columns)[:, None] - degrees) * np.arange(azimuths)[None, :]) % azimuths
    angle = 2.0 * np.pi * turns / azimuths
    cosine, sine = np.cos(angle), np.sin(angle)
    upper = np.concatenate([cosine, sine], axis=1)
    lower = np.concatenate([-sine, cosine], axis=1)
    return np.concatenate([upper, lower], axis=0).astype(np.float32)


def phase_tables(parts, azimuths):
    polar = np.pi * (np.arange(J) + 0.5) / J
    azimuth = 2.0 * np.pi * np.arange(azimuths) / azimuths
    octants = np.arange(8)
    sign = [(2 * (octants >> bit & 1) - 1).astype(np.float64)[:, None, None] for bit in range(3)]
    dir_x = np.sin(polar)[:, None] * np.cos(azimuth)[None, :]
    dir_y = np.sin(polar)[:, None] * np.sin(azimuth)[None, :]
    dir_z = np.cos(polar)[:, None] * np.ones_like(azimuth)[None, :]
    phase = 5.5 * (sign[0] * dir_x + sign[1] * dir_y + sign[2] * dir_z)

    def per_part(values):
        twice = np.repeat(values, 2, axis=1).astype(np.float32)
        return twice.reshape(8, parts, 2 * J // parts, azimuths).transpose(1, 0, 2, 3)

    return per_part(np.cos(phase)), per_part(np.sin(phase))


def pack(slot, source, out, placed, stage, count):
    step = pl.program_id(0)
    blk = lax.axis_index("blk")
    boxes, depth_lines, columns = source.shape
    sub_count, groups, rows, each, lines, _ = out.shape
    depth = depth_lines // lines
    total = sub_count * groups * each

    @pl.when(step == 0)
    def _():
        stage[...] = jnp.zeros_like(stage)
        placed[...] = jnp.zeros_like(placed)
        for sub in range(sub_count):
            count[sub] = 0

    lane = lax.broadcasted_iota(jnp.int32, (boxes, lines, columns), 2)
    for inner in range(depth):
        degree = depth * blk + inner
        begin = first_lane(depth, blk, inner)
        row, offset = begin // LANES, begin % LANES
        end = offset + 2 * degree + 1
        value = source[:, pl.ds(inner, lines, depth), :]
        value = pltpu.roll(value, (offset + LANES + degree - columns // 2) % LANES, 2)
        here = (lane >= offset) & (lane < end)
        stage[row] = jnp.where(here, value, stage[row])
        stage[row + 1] = jnp.where(lane < end - LANES, value, stage[row + 1])

    slot_lane = lax.broadcasted_iota(jnp.int32, (1, LANES), 1)
    for box in range(boxes):
        own = slot[step * boxes + box]
        target = own // total
        rank = count[target]
        count[target] = rank + 1
        out[target, rank // each, :, rank % each] = stage[pl.ds(0, rows), box]
        placed[target] = jnp.where(slot_lane == rank, own % total, placed[target])


def fill_table(tab, diag, cosines, order_ref, factor_ref, before_ref):
    degrees, width, lines, columns = tab.shape
    order = jnp.broadcast_to(order_ref[...], diag.shape)
    next_value = jnp.sqrt(2.0 * order + 3.0) * cosines * diag

    def advance(degree, state):
        previous, before = state
        level = lax.convert_element_type(degree, jnp.float32)
        recur = factor_ref[degree] * (cosines * previous - before * before_ref[degree])
        value = jnp.where(level == order + 1.0, next_value, recur)
        value = jnp.where(level == order, diag, value)
        value = jnp.where(level < order, 0.0, value)
        tab[degree] = jnp.broadcast_to(value[:, None, :], (width, lines, columns))
        return value, previous

    zeros = diag - diag
    lax.fori_loop(0, degrees, advance, (zeros, zeros))


def exchange(
    blocks,
    slots,
    diag,
    cosines,
    orders,
    factor,
    before,
    high,
    low,
    waves,
    quarters,
    source_of,
    placed,
    gathered,
    tab,
    cycles,
    send_far,
    recv_far,
    send_near,
    recv_near,
    send_pair,
    recv_pair,
    send_slot,
    recv_slot,
    local,
):
    sub_count, groups, _, each, lines, columns = blocks.shape
    degrees, width, _, _ = tab.shape
    parts = diag.shape[0]
    chips = parts // 2
    depth = degrees // parts
    cases = lines // 2
    sizes = [packed_rows(depth, part) for part in range(parts)]
    starts = [sum(sizes[:part]) for part in range(parts)]
    sub = lax.axis_index("sub")
    blk = lax.axis_index("blk")
    chip = blk // 2
    core = blk % 2
    sibling = chip * 2 + (1 - core)

    def start_of(part):
        total = 0
        for before_part in range(parts - 1):
            total = total + jnp.where(part > before_part, sizes[before_part], 0)
        return total

    def sized(part, action):
        rows = packed_rows(depth, part)
        for size in sorted(set(sizes)):
            pl.when(rows == size)(functools.partial(action, size))

    def remote(source, target, send, recv, device):
        return pltpu.make_async_remote_copy(
            src_ref=source,
            dst_ref=target,
            send_sem=send,
            recv_sem=recv,
            device_id=device,
            device_id_type=pl.DeviceIdType.MESH,
        )

    own_rows = start_of(blk)

    def held(hop, of_core):
        return ((chip + chips - hop) % chips) * 2 + of_core

    def far(step, group, size):
        peer = swapped(sub, step, sub_count)
        return remote(
            blocks.at[peer, group, pl.ds(0, size)],
            gathered.at[sub, group, pl.ds(own_rows, size)],
            send_far.at[step, group],
            recv_far.at[step, group],
            (peer, blk),
        )

    def slot_copy(step):
        peer = swapped(sub, step, sub_count)
        return remote(slots.at[peer], placed.at[sub], send_slot.at[step], recv_slot.at[step], (peer, blk))

    def near(hop, step, group, part, size, own=False):
        source = swapped(sub, step, sub_count)
        rows = pl.ds(start_of(part), size)
        return remote(
            blocks.at[sub, group, pl.ds(0, size)] if own else gathered.at[source, group, rows],
            gathered.at[source, group, rows],
            send_near.at[hop - 1, step, group],
            recv_near.at[hop - 1, step, group],
            (sub, ((chip + hop) % chips) * 2 + core),
        )

    def pair(hop, step, group, part, size, own=False):
        source = swapped(sub, step, sub_count)
        rows = pl.ds(start_of(part), size)
        return remote(
            blocks.at[sub, group, pl.ds(0, size)] if own else gathered.at[source, group, rows],
            gathered.at[source, group, rows],
            send_pair.at[hop, step, group],
            recv_pair.at[hop, step, group],
            (sub, sibling),
        )

    def keep(group, size):
        return pltpu.make_async_copy(
            blocks.at[sub, group, pl.ds(0, size)],
            gathered.at[sub, group, pl.ds(own_rows, size)],
            local.at[group],
        )

    barrier = pltpu.get_barrier_semaphore()

    def greet(device):
        pl.semaphore_signal(barrier, inc=1, device_id=device, device_id_type=pl.DeviceIdType.MESH)

    for step in range(1, sub_count):
        greet((swapped(sub, step, sub_count), blk))
    for hop in range(1, chips):
        greet((sub, ((chip + hop) % chips) * 2 + core))
    greet((sub, sibling))
    pl.semaphore_wait(barrier, sub_count - 1 + chips)

    others = sub_count - 1

    def step_at(index):
        return 1 + (index + sub_count // 2 - 1) % others

    for step in range(1, sub_count):
        slot_copy(step).start()
    keep_slot = pltpu.make_async_copy(slots.at[sub], placed.at[sub], local.at[groups])
    keep_slot.start()

    def begin(size):
        @pl.loop(0, groups)
        def _(group):
            for hop in range(1, chips):
                near(hop, 0, group, blk, size, True).start()

            @pl.loop(0, others)
            def _(index):
                far(step_at(index), group, size).start()

            pair(0, 0, group, blk, size, True).start()
            keep(group, size).start()

    sized(blk, begin)
    fill_table(tab, diag[blk], cosines[blk], orders, factor, before)

    lane = lax.broadcasted_iota(jnp.int32, (each, lines, columns), 2)

    def relay(step, group):
        def act(size):
            far(step, group, size).wait_recv()
            for hop in range(1, chips):
                near(hop, step, group, blk, size).start()
            pair(0, step, group, blk, size).start()

        sized(blk, act)

    def hand_on(step, group):
        for hop in range(1, chips):
            part = held(hop, core)

            def act(size):
                near(hop, step, group, part, size).wait_recv()
                pair(hop, step, group, part, size).start()

            sized(part, act)

    def finish(step, group):
        for hop in range(chips):
            part = held(hop, 1 - core)
            sized(part, lambda size: pair(hop, step, group, part, size).wait_recv())
        source = swapped(sub, step, sub_count)
        totals = [jnp.zeros((width, lines, columns), jnp.float32) for _ in range(each)]
        for degree in range(degrees):
            part, inner = degree // depth, degree % depth
            begin = first_lane(depth, part, inner)
            row, offset = starts[part] + begin // LANES, begin % LANES
            value = gathered[source, group, row]
            if offset + 2 * degree + 1 > LANES:
                value = jnp.where(lane >= offset, value, gathered[source, group, row + 1])
            shift = (columns // 2 - degree - offset) % LANES
            if shift:
                value = pltpu.roll(value, shift, 2)
            for box in range(each):
                totals[box] = totals[box] + value[box][None] * tab[degree]
        for box in range(each):
            for index in range(width):
                cycles[pl.ds(box * lines * width + index, lines, width), :] = totals[box][index]
        both = cycles[...].reshape(each * cases, 2, width, columns)
        rows = each * cases * width
        both = jnp.concatenate([both[:, 0].reshape(rows, columns), both[:, 1].reshape(rows, columns)], axis=1)
        top = both.astype(jnp.bfloat16)
        rest = (both - top.astype(jnp.float32)).astype(jnp.bfloat16)
        dot = functools.partial(jnp.dot, preferred_element_type=jnp.float32)
        wave = dot(rest, high[...]) + dot(top, low[...]) + dot(top, high[...])
        real, imag = wave[:, :K], wave[:, K:]
        for box in range(each):
            for case in range(cases):
                at = slice((box * cases + case) * width, (box * cases + case + 1) * width)
                waves[source, group, box, case, pl.ds(0, width, 2), :] = real[at]
                waves[source, group, box, case, pl.ds(1, width, 2), :] = imag[at]
                quarters[source, group, box, case, pl.ds(0, width, 2), :] = -imag[at]
                quarters[source, group, box, case, pl.ds(1, width, 2), :] = real[at]

    def waits_keep(size):
        @pl.loop(0, groups)
        def _(group):
            keep(group, size).wait()

    sized(blk, waits_keep)

    chunks = sub_count * groups
    near_lag, pair_lag = 2, 4

    def place_of(chunk):
        later = chunk - groups
        own = chunk < groups
        step = jnp.where(own, 0, step_at(later % others))
        group = jnp.where(own, chunk, later // others)
        return step, group

    @pl.loop(0, chunks + pair_lag)
    def _(chunk):
        @pl.when((chunk >= groups) & (chunk < chunks))
        def _():
            relay(*place_of(chunk))

        @pl.when(chunk >= pair_lag)
        def _():
            finish(*place_of(chunk - pair_lag))

        @pl.when((chunk >= near_lag) & (chunk < chunks + near_lag))
        def _():
            hand_on(*place_of(chunk - near_lag))

    def drain(step, group):
        def own_act(size):
            @pl.when(step > 0)
            def _():
                far(step, group, size).wait_send()

            for hop in range(1, chips):
                near(hop, step, group, blk, size).wait_send()
            pair(0, step, group, blk, size).wait_send()

        sized(blk, own_act)
        for hop in range(1, chips):
            part = held(hop, core)
            sized(part, lambda size: pair(hop, step, group, part, size).wait_send())

    @pl.loop(0, chunks)
    def _(chunk):
        drain(*place_of(chunk))

    for step in range(1, sub_count):
        slot_copy(step).wait()
    keep_slot.wait()
    per_peer = groups * each
    turned = jnp.transpose(placed[:, 0, :])
    where = lax.broadcasted_iota(jnp.int32, (per_peer, LANES), 1)
    rank = lax.broadcasted_iota(jnp.int32, (per_peer, LANES), 0)
    found = jnp.zeros((1, LANES), jnp.int32)
    for source in range(sub_count):
        slot = turned[:per_peer, source : source + 1]
        hit = jnp.where(slot == where, rank + source * per_peer, 0)
        found = found + jnp.sum(hit, axis=0, keepdims=True)
    source_of[...] = found


def phases(source_of, octants, waves, quarters, phase_cos, phase_sin, out):
    step = pl.program_id(0)
    count, cases, places, _, _ = out.shape
    for box in range(count):
        at = step * count + box
        source = source_of[at]
        for place in range(places):
            octant = octants[place, at]
            turn_cos = phase_cos[0, octant]
            turn_sin = phase_sin[0, octant]
            for case in range(cases):
                out[box, case, place] = waves[source, case] * turn_cos + quarters[source, case] * turn_sin


def body(coefficients, owner_slot, child_list):
    boxes, cases, _, depth, columns = coefficients.shape
    sub_count = lax.axis_size("sub")
    parts = lax.axis_size("blk")
    degrees = parts * depth
    width = J // parts
    lines = cases * 2
    per_peer = boxes // sub_count
    each = 2 if per_peer % 2 == 0 else 1
    groups = per_peer // each
    chips = parts // 2
    hops = max(chips - 1, 1)
    rows = max(packed_rows(depth, part) for part in range(parts))
    total_rows = sum(packed_rows(depth, part) for part in range(parts))
    vmem = pl.BlockSpec(memory_space=pltpu.VMEM)
    at_once = 8
    outgoing, slots = pl.pallas_call(
        pack,
        grid_spec=pltpu.PrefetchScalarGridSpec(
            num_scalar_prefetch=1,
            grid=(boxes // at_once,),
            in_specs=[pl.BlockSpec((at_once, lines * depth, columns), lambda i, slot: (i, 0, 0))],
            out_specs=(vmem, vmem),
            scratch_shapes=[
                pltpu.VMEM((rows + 1, at_once, lines, columns), jnp.float32),
                pltpu.SMEM((sub_count,), jnp.int32),
            ],
        ),
        out_shape=(
            jax.ShapeDtypeStruct((sub_count, groups, rows, each, lines, columns), jnp.float32),
            jax.ShapeDtypeStruct((sub_count, 1, LANES), jnp.int32),
        ),
        compiler_params=pltpu.CompilerParams(vmem_limit_bytes=12 * MIB),
        name="pack",
    )(owner_slot, coefficients.reshape(boxes, lines * depth, columns))

    matrix = wave_matrix(degrees, columns, K)
    high = matrix.astype(jnp.bfloat16)
    low = (matrix - high.astype(np.float32)).astype(jnp.bfloat16)
    dma = pltpu.SemaphoreType.DMA
    waves, quarters, source_of = pl.pallas_call(
        exchange,
        out_shape=(
            jax.ShapeDtypeStruct((sub_count, groups, each, cases, 2 * width, K), jnp.float32),
            jax.ShapeDtypeStruct((sub_count, groups, each, cases, 2 * width, K), jnp.float32),
            jax.ShapeDtypeStruct((1, LANES), jnp.int32),
        ),
        in_specs=[vmem] * 9,
        out_specs=(vmem, vmem, vmem),
        scratch_shapes=[
            pltpu.VMEM((sub_count, 1, LANES), jnp.int32),
            pltpu.VMEM((sub_count, groups, total_rows, each, lines, columns), jnp.float32),
            pltpu.VMEM((degrees, width, lines, columns), jnp.float32),
            pltpu.VMEM((each * lines * width, columns), jnp.float32),
            dma((sub_count, groups)),
            dma((sub_count, groups)),
            dma((hops, sub_count, groups)),
            dma((hops, sub_count, groups)),
            dma((chips, sub_count, groups)),
            dma((chips, sub_count, groups)),
            dma((sub_count,)),
            dma((sub_count,)),
            dma((groups + 1,)),
        ],
        compiler_params=pltpu.CompilerParams(
            collective_id=0, has_side_effects=True, vmem_limit_bytes=40 * MIB
        ),
        name="exchange",
    )(
        outgoing,
        slots,
        *(jnp.asarray(constant) for constant in legendre_constants(degrees, columns, parts)),
        jnp.asarray(high),
        jnp.asarray(low),
    )

    phase_cos, phase_sin = phase_tables(parts, K)
    blk = lax.axis_index("blk").astype(jnp.int32)
    count = 2
    own = pl.BlockSpec((1, 8, 2 * width, K), lambda i, source, octants, part: (part[0], 0, 0, 0))
    out = pl.pallas_call(
        lambda source, octants, part, *refs: phases(source, octants, *refs),
        grid_spec=pltpu.PrefetchScalarGridSpec(
            num_scalar_prefetch=3,
            grid=(boxes // count,),
            in_specs=[vmem, vmem, own, own],
            out_specs=pl.BlockSpec(
                (count, cases, 8, 2 * width, K), lambda i, source, octants, part: (i, 0, 0, 0, 0)
            ),
        ),
        out_shape=jax.ShapeDtypeStruct((boxes, cases, 8, 2 * width, K), jnp.float32),
        compiler_params=pltpu.CompilerParams(vmem_limit_bytes=32 * MIB),
        name="phases",
    )(
        source_of.reshape(-1),
        child_list.T,
        blk.reshape(1),
        waves.reshape(boxes, cases, 2 * width, K),
        quarters.reshape(boxes, cases, 2 * width, K),
        jnp.asarray(phase_cos),
        jnp.asarray(phase_sin),
    )
    return out.reshape(boxes, cases, 8, width, 2, K)


def solution(mesh):
    placed = (P("sub", None, None, "blk", None), P("sub"), P("sub", None))
    return jax.shard_map(
        body,
        mesh=mesh,
        in_specs=placed,
        out_specs=P("sub", None, None, "blk", None, None),
        check_vma=False,
    )
```

```python
import functools
import math

import jax
import jax.numpy as jnp
import numpy as np
from jax import lax
from jax.experimental import pallas as pl
from jax.experimental.pallas import tpu as pltpu
from jax.sharding import PartitionSpec as P

J = 64
K = 128
LANES = 128
MIB = 1024 * 1024


def ceil_div(value, by):
    return (value + by - 1) // by


def packed_rows(depth, part):
    return ceil_div(depth * depth * (2 * part + 1), LANES)


def first_lane(depth, part, inner):
    return inner * (2 * depth * part) + inner * inner


def swapped(index, step, size):
    total = 0
    bit = 1
    while bit < size:
        total = total + ((index // bit + step // bit) % 2) * bit
        bit *= 2
    return total


def legendre_constants(degrees, columns, parts):
    order = np.abs(np.arange(columns) - degrees).astype(np.float64)
    log_norm = np.array(
        [
            0.5
            * (
                math.log((2 * v + 1) / (4 * math.pi))
                + math.lgamma(2 * v + 1)
                - v * math.log(4.0)
                - 2 * math.lgamma(v + 1)
            )
            for v in order
        ]
    )
    polar = np.pi * (np.arange(J) + 0.5) / J
    diag = np.exp(log_norm[None] + order[None] * np.log(np.sin(polar))[:, None])
    cosines = np.broadcast_to(np.cos(polar)[:, None], (J, columns))
    level = np.arange(degrees, dtype=np.float64)[:, None]
    factor = np.sqrt(np.maximum(4 * level * level - 1, 1.0) / np.maximum(level * level - order[None] ** 2, 1.0))
    before = np.ones_like(factor)
    before[1:] = 1.0 / factor[:-1]
    shape = (parts, J // parts, columns)
    return (
        diag.astype(np.float32).reshape(shape),
        cosines.astype(np.float32).reshape(shape),
        order.astype(np.float32)[None],
        factor.astype(np.float32)[:, None, :],
        before.astype(np.float32)[:, None, :],
    )


def wave_matrix(degrees, columns, azimuths):
    turns = ((np.arange(columns)[:, None] - degrees) * np.arange(azimuths)[None, :]) % azimuths
    angle = 2.0 * np.pi * turns / azimuths
    cosine, sine = np.cos(angle), np.sin(angle)
    upper = np.concatenate([cosine, sine], axis=1)
    lower = np.concatenate([-sine, cosine], axis=1)
    return np.concatenate([upper, lower], axis=0).astype(np.float32)


def phase_tables(parts, azimuths):
    polar = np.pi * (np.arange(J) + 0.5) / J
    azimuth = 2.0 * np.pi * np.arange(azimuths) / azimuths
    octants = np.arange(8)
    sign = [(2 * (octants >> bit & 1) - 1).astype(np.float64)[:, None, None] for bit in range(3)]
    dir_x = np.sin(polar)[:, None] * np.cos(azimuth)[None, :]
    dir_y = np.sin(polar)[:, None] * np.sin(azimuth)[None, :]
    dir_z = np.cos(polar)[:, None] * np.ones_like(azimuth)[None, :]
    phase = 5.5 * (sign[0] * dir_x + sign[1] * dir_y + sign[2] * dir_z)

    def per_part(values):
        twice = np.repeat(values, 2, axis=1).astype(np.float32)
        return twice.reshape(8, parts, 2 * J // parts, azimuths).transpose(1, 0, 2, 3)

    return per_part(np.cos(phase)), per_part(np.sin(phase))


def pack(slot, source, out, placed, stage, count, arrived, sems):
    blk = lax.axis_index("blk")
    _, at_once, depth_lines, columns = arrived.shape
    sub_count, groups, rows, each, lines, _ = out.shape
    depth = depth_lines // lines
    total = sub_count * groups * each
    steps = total // at_once

    def fetch(step):
        return pltpu.make_async_copy(source.at[pl.ds(step * at_once, at_once)], arrived.at[step], sems.at[step])

    for step in range(steps):
        fetch(step).start()
    stage[...] = jnp.zeros_like(stage)
    placed[...] = jnp.zeros_like(placed)
    for sub in range(sub_count):
        count[sub] = 0
    lane = lax.broadcasted_iota(jnp.int32, (at_once, lines, columns), 2)
    slot_lane = lax.broadcasted_iota(jnp.int32, (1, LANES), 1)

    @pl.loop(0, steps)
    def _(step):
        fetch(step).wait()
        for inner in range(depth):
            degree = depth * blk + inner
            begin = first_lane(depth, blk, inner)
            row, offset = begin // LANES, begin % LANES
            end = offset + 2 * degree + 1
            value = arrived[step, :, pl.ds(inner, lines, depth), :]
            value = pltpu.roll(value, (offset + LANES + degree - columns // 2) % LANES, 2)
            here = (lane >= offset) & (lane < end)
            stage[row] = jnp.where(here, value, stage[row])
            stage[row + 1] = jnp.where(lane < end - LANES, value, stage[row + 1])
        for box in range(at_once):
            own = slot[step * at_once + box]
            target = own // total
            rank = count[target]
            count[target] = rank + 1
            out[target, rank // each, :, rank % each] = stage[pl.ds(0, rows), box]
            placed[target] = jnp.where(slot_lane == rank, own % total, placed[target])


def fill_table(tab, diag, cosines, order_ref, factor_ref, before_ref):
    degrees, width, lines, columns = tab.shape
    order = jnp.broadcast_to(order_ref[...], diag.shape)
    next_value = jnp.sqrt(2.0 * order + 3.0) * cosines * diag

    def advance(degree, state):
        previous, before = state
        level = lax.convert_element_type(degree, jnp.float32)
        recur = factor_ref[degree] * (cosines * previous - before * before_ref[degree])
        value = jnp.where(level == order + 1.0, next_value, recur)
        value = jnp.where(level == order, diag, value)
        value = jnp.where(level < order, 0.0, value)
        tab[degree] = jnp.broadcast_to(value[:, None, :], (width, lines, columns))
        return value, previous

    zeros = diag - diag
    lax.fori_loop(0, degrees, advance, (zeros, zeros))


def exchange(
    blocks,
    slots,
    diag,
    cosines,
    orders,
    factor,
    before,
    high,
    low,
    waves,
    quarters,
    source_of,
    placed,
    gathered,
    tab,
    cycles,
    send_far,
    recv_far,
    send_near,
    recv_near,
    send_pair,
    recv_pair,
    send_slot,
    recv_slot,
    local,
    transit,
    send_early,
    recv_early,
    send_far2,
    recv_far2,
):
    sub_count, groups, _, each, lines, columns = blocks.shape
    degrees, width, _, _ = tab.shape
    parts = diag.shape[0]
    chips = parts // 2
    depth = degrees // parts
    cases = lines // 2
    sizes = [packed_rows(depth, part) for part in range(parts)]
    starts = [sum(sizes[:part]) for part in range(parts)]
    sub = lax.axis_index("sub")
    blk = lax.axis_index("blk")
    chip = blk // 2
    core = blk % 2
    sibling = chip * 2 + (1 - core)

    def start_of(part):
        total = 0
        for before_part in range(parts - 1):
            total = total + jnp.where(part > before_part, sizes[before_part], 0)
        return total

    def sized(part, action):
        rows = packed_rows(depth, part)
        for size in sorted(set(sizes)):
            pl.when(rows == size)(functools.partial(action, size))

    def remote(source, target, send, recv, device):
        return pltpu.make_async_remote_copy(
            src_ref=source,
            dst_ref=target,
            send_sem=send,
            recv_sem=recv,
            device_id=device,
            device_id_type=pl.DeviceIdType.MESH,
        )

    own_rows = start_of(blk)
    feeds = blk == parts - 1 if chips == 2 else None
    forwards = blk == parts - 3 if chips == 2 else None
    heavy, heavy_rows = sizes[-1], starts[-1]

    def early(step, group):
        peer = swapped(sub, step, sub_count)
        return remote(
            blocks.at[peer, group, pl.ds(0, heavy)],
            transit.at[step, group],
            send_early.at[step, group],
            recv_early.at[step, group],
            (sub, parts - 3),
        )

    def far2(step, group):
        peer = swapped(sub, step, sub_count)
        return remote(
            transit.at[step, group],
            gathered.at[sub, group, pl.ds(heavy_rows, heavy)],
            send_far2.at[step, group],
            recv_far2.at[step, group],
            (peer, blk),
        )

    def held(hop, of_core):
        return ((chip + chips - hop) % chips) * 2 + of_core

    def far(step, group, size):
        peer = swapped(sub, step, sub_count)
        return remote(
            blocks.at[peer, group, pl.ds(0, size)],
            gathered.at[sub, group, pl.ds(own_rows, size)],
            send_far.at[step, group],
            recv_far.at[step, group],
            (peer, blk),
        )

    def slot_copy(step):
        peer = swapped(sub, step, sub_count)
        return remote(slots.at[peer], placed.at[sub], send_slot.at[step], recv_slot.at[step], (peer, blk))

    def near(hop, step, group, part, size, own=False):
        source = swapped(sub, step, sub_count)
        rows = pl.ds(start_of(part), size)
        return remote(
            blocks.at[sub, group, pl.ds(0, size)] if own else gathered.at[source, group, rows],
            gathered.at[source, group, rows],
            send_near.at[hop - 1, step, group],
            recv_near.at[hop - 1, step, group],
            (sub, ((chip + hop) % chips) * 2 + core),
        )

    def pair(hop, step, group, part, size, own=False):
        source = swapped(sub, step, sub_count)
        rows = pl.ds(start_of(part), size)
        return remote(
            blocks.at[sub, group, pl.ds(0, size)] if own else gathered.at[source, group, rows],
            gathered.at[source, group, rows],
            send_pair.at[hop, step, group],
            recv_pair.at[hop, step, group],
            (sub, sibling),
        )

    def keep(group, size):
        return pltpu.make_async_copy(
            blocks.at[sub, group, pl.ds(0, size)],
            gathered.at[sub, group, pl.ds(own_rows, size)],
            local.at[group],
        )

    barrier = pltpu.get_barrier_semaphore()

    def greet(device):
        pl.semaphore_signal(barrier, inc=1, device_id=device, device_id_type=pl.DeviceIdType.MESH)

    for step in range(1, sub_count):
        greet((swapped(sub, step, sub_count), blk))
    for hop in range(1, chips):
        greet((sub, ((chip + hop) % chips) * 2 + core))
    greet((sub, sibling))
    pl.semaphore_wait(barrier, sub_count - 1 + chips)

    others = sub_count - 1
    ahead = 1

    def step_at(index):
        return 1 + (index + sub_count // 2 - 1) % others

    for step in range(1, sub_count):
        slot_copy(step).start()
    keep_slot = pltpu.make_async_copy(slots.at[sub], placed.at[sub], local.at[groups])
    keep_slot.start()

    def begin(size):
        @pl.loop(0, min(ahead, groups))
        def _(group):
            @pl.loop(0, others)
            def _(index):
                far(step_at(index), group, size).start()

        @pl.loop(0, groups)
        def _(group):
            for hop in range(1, chips):
                near(hop, 0, group, blk, size, True).start()

            pair(0, 0, group, blk, size, True).start()
            keep(group, size).start()

    sized(blk, begin)
    if chips == 2:

        @pl.when(feeds)
        def _():
            @pl.loop(0, groups)
            def _(group):
                @pl.loop(0, others)
                def _(index):
                    early(step_at(index), group).start()

    fill_table(tab, diag[blk], cosines[blk], orders, factor, before)

    lane = lax.broadcasted_iota(jnp.int32, (each, lines, columns), 2)

    def relay(step, group):
        def act(size):
            far(step, group, size).wait_recv()
            if chips != 2:
                for hop in range(1, chips):
                    near(hop, step, group, blk, size).start()
            elif size != heavy:
                near(1, step, group, blk, size).start()
            pair(0, step, group, blk, size).start()

            @pl.when(group + ahead < groups)
            def _():
                far(step, group + ahead, size).start()

        sized(blk, act)

    def forward(step, group):
        @pl.when(forwards)
        def _():
            early(step, group).wait_recv()
            far2(step, group).start()

    def hand_on(step, group):
        for hop in range(1, chips):
            part = held(hop, core)

            def act(size):
                if chips == 2 and size == heavy:

                    @pl.when(step > 0)
                    def _():
                        far2(step, group).wait_recv()

                    @pl.when(step == 0)
                    def _():
                        near(hop, step, group, part, size).wait_recv()

                else:
                    near(hop, step, group, part, size).wait_recv()
                pair(hop, step, group, part, size).start()

            sized(part, act)

    def finish(step, group):
        for hop in range(chips):
            part = held(hop, 1 - core)
            sized(part, lambda size: pair(hop, step, group, part, size).wait_recv())
        source = swapped(sub, step, sub_count)
        totals = [jnp.zeros((width, lines, columns), jnp.float32) for _ in range(each)]
        for degree in range(degrees):
            part, inner = degree // depth, degree % depth
            begin = first_lane(depth, part, inner)
            row, offset = starts[part] + begin // LANES, begin % LANES
            value = gathered[source, group, row]
            if offset + 2 * degree + 1 > LANES:
                value = jnp.where(lane >= offset, value, gathered[source, group, row + 1])
            shift = (columns // 2 - degree - offset) % LANES
            if shift:
                value = pltpu.roll(value, shift, 2)
            for box in range(each):
                totals[box] = totals[box] + value[box][None] * tab[degree]
        for box in range(each):
            for index in range(width):
                cycles[pl.ds(box * lines * width + index, lines, width), :] = totals[box][index]
        both = cycles[...].reshape(each * cases, 2, width, columns)
        rows = each * cases * width
        both = jnp.concatenate([both[:, 0].reshape(rows, columns), both[:, 1].reshape(rows, columns)], axis=1)
        top = both.astype(jnp.bfloat16)
        rest = (both - top.astype(jnp.float32)).astype(jnp.bfloat16)
        dot = functools.partial(jnp.dot, preferred_element_type=jnp.float32)
        wave = dot(rest, high[...]) + dot(top, low[...]) + dot(top, high[...])
        real, imag = wave[:, :K], wave[:, K:]
        for box in range(each):
            for case in range(cases):
                at = slice((box * cases + case) * width, (box * cases + case + 1) * width)
                waves[source, group, box, case, pl.ds(0, width, 2), :] = real[at]
                waves[source, group, box, case, pl.ds(1, width, 2), :] = imag[at]
                quarters[source, group, box, case, pl.ds(0, width, 2), :] = -imag[at]
                quarters[source, group, box, case, pl.ds(1, width, 2), :] = real[at]

    def waits_keep(size):
        @pl.loop(0, groups)
        def _(group):
            keep(group, size).wait()

    sized(blk, waits_keep)

    chunks = sub_count * groups
    near_lag, pair_lag = 3, 5

    def place_of(chunk):
        later = chunk - groups
        own = chunk < groups
        step = jnp.where(own, 0, step_at(later % others))
        group = jnp.where(own, chunk, later // others)
        return step, group

    @pl.loop(0, chunks + pair_lag)
    def _(chunk):
        @pl.when((chunk >= groups) & (chunk < chunks))
        def _():
            relay(*place_of(chunk))
            if chips == 2:
                forward(*place_of(chunk))

        @pl.when(chunk >= pair_lag)
        def _():
            finish(*place_of(chunk - pair_lag))

        @pl.when((chunk >= near_lag) & (chunk < chunks + near_lag))
        def _():
            hand_on(*place_of(chunk - near_lag))

    def drain(step, group):
        def own_act(size):
            @pl.when(step > 0)
            def _():
                far(step, group, size).wait_send()

            if chips == 2 and size == heavy:

                @pl.when(step > 0)
                def _():
                    early(step, group).wait_send()

                @pl.when(step == 0)
                def _():
                    near(1, step, group, blk, size).wait_send()

            else:
                for hop in range(1, chips):
                    near(hop, step, group, blk, size).wait_send()
            pair(0, step, group, blk, size).wait_send()

        sized(blk, own_act)
        if chips == 2:

            @pl.when(forwards & (step > 0))
            def _():
                far2(step, group).wait_send()

        for hop in range(1, chips):
            part = held(hop, core)
            sized(part, lambda size: pair(hop, step, group, part, size).wait_send())

    @pl.loop(0, chunks)
    def _(chunk):
        drain(*place_of(chunk))

    for step in range(1, sub_count):
        slot_copy(step).wait()
    keep_slot.wait()
    per_peer = groups * each
    turned = jnp.transpose(placed[:, 0, :])
    where = lax.broadcasted_iota(jnp.int32, (per_peer, LANES), 1)
    rank = lax.broadcasted_iota(jnp.int32, (per_peer, LANES), 0)
    found = jnp.zeros((1, LANES), jnp.int32)
    for source in range(sub_count):
        slot = turned[:per_peer, source : source + 1]
        hit = jnp.where(slot == where, rank + source * per_peer, 0)
        found = found + jnp.sum(hit, axis=0, keepdims=True)
    source_of[...] = found


def phases(source_of, octants, waves, quarters, phase_cos, phase_sin, out, blocks, sems):
    slots, count, cases, places, _, _ = blocks.shape
    boxes = out.shape[0]

    def send(step):
        slot = step % slots
        return pltpu.make_async_copy(blocks.at[slot], out.at[pl.ds(step * count, count)], sems.at[slot])

    @pl.loop(0, boxes // count)
    def _(step):
        slot = step % slots

        @pl.when(step >= slots)
        def _():
            send(step - slots).wait()

        for box in range(count):
            at = step * count + box
            source = source_of[at]
            for place in range(places):
                octant = octants[place, at]
                turn_cos = phase_cos[0, octant]
                turn_sin = phase_sin[0, octant]
                for case in range(cases):
                    blocks[slot, box, case, place] = waves[source, case] * turn_cos + quarters[source, case] * turn_sin
        send(step).start()

    @pl.loop(boxes // count - slots, boxes // count)
    def _(step):
        send(step).wait()


def body(coefficients, owner_slot, child_list):
    boxes, cases, _, depth, columns = coefficients.shape
    sub_count = lax.axis_size("sub")
    parts = lax.axis_size("blk")
    degrees = parts * depth
    width = J // parts
    lines = cases * 2
    per_peer = boxes // sub_count
    each = 2 if per_peer % 2 == 0 else 1
    groups = per_peer // each
    chips = parts // 2
    hops = max(chips - 1, 1)
    rows = max(packed_rows(depth, part) for part in range(parts))
    total_rows = sum(packed_rows(depth, part) for part in range(parts))
    vmem = pl.BlockSpec(memory_space=pltpu.VMEM)
    dma = pltpu.SemaphoreType.DMA
    at_once = 8
    outgoing, slots = pl.pallas_call(
        pack,
        grid_spec=pltpu.PrefetchScalarGridSpec(
            num_scalar_prefetch=1,
            grid=(1,),
            in_specs=[pl.BlockSpec(memory_space=pltpu.HBM)],
            out_specs=(vmem, vmem),
            scratch_shapes=[
                pltpu.VMEM((rows + 1, at_once, lines, columns), jnp.float32),
                pltpu.SMEM((sub_count,), jnp.int32),
                pltpu.VMEM((boxes // at_once, at_once, lines * depth, columns), jnp.float32),
                dma((boxes // at_once,)),
            ],
        ),
        out_shape=(
            jax.ShapeDtypeStruct((sub_count, groups, rows, each, lines, columns), jnp.float32),
            jax.ShapeDtypeStruct((sub_count, 1, LANES), jnp.int32),
        ),
        compiler_params=pltpu.CompilerParams(vmem_limit_bytes=16 * MIB),
        name="pack",
    )(owner_slot, coefficients.reshape(boxes, lines * depth, columns))

    matrix = wave_matrix(degrees, columns, K)
    high = matrix.astype(jnp.bfloat16)
    low = (matrix - high.astype(np.float32)).astype(jnp.bfloat16)
    waves, quarters, source_of = pl.pallas_call(
        exchange,
        out_shape=(
            jax.ShapeDtypeStruct((sub_count, groups, each, cases, 2 * width, K), jnp.float32),
            jax.ShapeDtypeStruct((sub_count, groups, each, cases, 2 * width, K), jnp.float32),
            jax.ShapeDtypeStruct((1, LANES), jnp.int32),
        ),
        in_specs=[vmem] * 9,
        out_specs=(vmem, vmem, vmem),
        scratch_shapes=[
            pltpu.VMEM((sub_count, 1, LANES), jnp.int32),
            pltpu.VMEM((sub_count, groups, total_rows, each, lines, columns), jnp.float32),
            pltpu.VMEM((degrees, width, lines, columns), jnp.float32),
            pltpu.VMEM((each * lines * width, columns), jnp.float32),
            dma((sub_count, groups)),
            dma((sub_count, groups)),
            dma((hops, sub_count, groups)),
            dma((hops, sub_count, groups)),
            dma((chips, sub_count, groups)),
            dma((chips, sub_count, groups)),
            dma((sub_count,)),
            dma((sub_count,)),
            dma((groups + 1,)),
            pltpu.VMEM((sub_count, groups, rows, each, lines, columns) if chips == 2 else (8, LANES), jnp.float32),
            dma((sub_count, groups)),
            dma((sub_count, groups)),
            dma((sub_count, groups)),
            dma((sub_count, groups)),
        ],
        compiler_params=pltpu.CompilerParams(
            collective_id=0, has_side_effects=True, vmem_limit_bytes=40 * MIB
        ),
        name="exchange",
    )(
        outgoing,
        slots,
        *(jnp.asarray(constant) for constant in legendre_constants(degrees, columns, parts)),
        jnp.asarray(high),
        jnp.asarray(low),
    )

    phase_cos, phase_sin = phase_tables(parts, K)
    blk = lax.axis_index("blk").astype(jnp.int32)
    count = 2 if boxes % 2 == 0 else 1
    slots = min(6, boxes // count)
    own = pl.BlockSpec((1, 8, 2 * width, K), lambda i, source, octants, part: (part[0], 0, 0, 0))
    out = pl.pallas_call(
        lambda source, octants, part, *refs: phases(source, octants, *refs),
        grid_spec=pltpu.PrefetchScalarGridSpec(
            num_scalar_prefetch=3,
            grid=(1,),
            in_specs=[vmem, vmem, own, own],
            out_specs=pl.BlockSpec(memory_space=pltpu.HBM),
            scratch_shapes=[
                pltpu.VMEM((slots, count, cases, 8, 2 * width, K), jnp.float32),
                dma((slots,)),
            ],
        ),
        out_shape=jax.ShapeDtypeStruct((boxes, cases, 8, 2 * width, K), jnp.float32),
        compiler_params=pltpu.CompilerParams(vmem_limit_bytes=32 * MIB),
        name="phases",
    )(
        source_of.reshape(-1),
        child_list.T,
        blk.reshape(1),
        waves.reshape(boxes, cases, 2 * width, K),
        quarters.reshape(boxes, cases, 2 * width, K),
        jnp.asarray(phase_cos),
        jnp.asarray(phase_sin),
    )
    return out.reshape(boxes, cases, 8, width, 2, K)


def solution(mesh):
    placed = (P("sub", None, None, "blk", None), P("sub"), P("sub", None))
    return jax.shard_map(
        body,
        mesh=mesh,
        in_specs=placed,
        out_specs=P("sub", None, None, "blk", None, None),
        check_vma=False,
    )
```

```python
import functools
import math

import jax
import jax.numpy as jnp
import numpy as np
from jax import lax
from jax.experimental import pallas as pl
from jax.experimental.pallas import tpu as pltpu
from jax.sharding import PartitionSpec as P

J = 64
K = 128
LANES = 128
MIB = 1024 * 1024


def ceil_div(value, by):
    return (value + by - 1) // by


def packed_rows(depth, part):
    return ceil_div(depth * depth * (2 * part + 1), LANES)


def first_lane(depth, part, inner):
    return inner * (2 * depth * part) + inner * inner


def swapped(index, step, size):
    total = 0
    bit = 1
    while bit < size:
        total = total + ((index // bit + step // bit) % 2) * bit
        bit *= 2
    return total


def legendre_constants(degrees, columns, parts):
    order = np.abs(np.arange(columns) - degrees).astype(np.float64)
    log_norm = np.array(
        [
            0.5
            * (
                math.log((2 * v + 1) / (4 * math.pi))
                + math.lgamma(2 * v + 1)
                - v * math.log(4.0)
                - 2 * math.lgamma(v + 1)
            )
            for v in order
        ]
    )
    polar = np.pi * (np.arange(J) + 0.5) / J
    diag = np.exp(log_norm[None] + order[None] * np.log(np.sin(polar))[:, None])
    cosines = np.broadcast_to(np.cos(polar)[:, None], (J, columns))
    level = np.arange(degrees, dtype=np.float64)[:, None]
    factor = np.sqrt(np.maximum(4 * level * level - 1, 1.0) / np.maximum(level * level - order[None] ** 2, 1.0))
    before = np.ones_like(factor)
    before[1:] = 1.0 / factor[:-1]
    shape = (parts, J // parts, columns)
    return (
        diag.astype(np.float32).reshape(shape),
        cosines.astype(np.float32).reshape(shape),
        order.astype(np.float32)[None],
        factor.astype(np.float32)[:, None, :],
        before.astype(np.float32)[:, None, :],
    )


def wave_matrix(degrees, columns, azimuths):
    turns = ((np.arange(columns)[:, None] - degrees) * np.arange(azimuths)[None, :]) % azimuths
    angle = 2.0 * np.pi * turns / azimuths
    cosine, sine = np.cos(angle), np.sin(angle)
    upper = np.concatenate([cosine, sine], axis=1)
    lower = np.concatenate([-sine, cosine], axis=1)
    return np.concatenate([upper, lower], axis=0).astype(np.float32)


def phase_tables(parts, azimuths):
    polar = np.pi * (np.arange(J) + 0.5) / J
    azimuth = 2.0 * np.pi * np.arange(azimuths) / azimuths
    octants = np.arange(8)
    sign = [(2 * (octants >> bit & 1) - 1).astype(np.float64)[:, None, None] for bit in range(3)]
    dir_x = np.sin(polar)[:, None] * np.cos(azimuth)[None, :]
    dir_y = np.sin(polar)[:, None] * np.sin(azimuth)[None, :]
    dir_z = np.cos(polar)[:, None] * np.ones_like(azimuth)[None, :]
    phase = 5.5 * (sign[0] * dir_x + sign[1] * dir_y + sign[2] * dir_z)

    def per_part(values):
        twice = np.repeat(values, 2, axis=1).astype(np.float32)
        return twice.reshape(8, parts, 2 * J // parts, azimuths).transpose(1, 0, 2, 3)

    return per_part(np.cos(phase)), per_part(np.sin(phase))


def pack(slot, source, out, placed, stage, count, arrived, sems):
    blk = lax.axis_index("blk")
    _, at_once, depth_lines, columns = arrived.shape
    sub_count, groups, rows, each, lines, _ = out.shape
    depth = depth_lines // lines
    total = sub_count * groups * each
    steps = total // at_once

    def fetch(step):
        return pltpu.make_async_copy(source.at[pl.ds(step * at_once, at_once)], arrived.at[step], sems.at[step])

    for step in range(steps):
        fetch(step).start()
    stage[...] = jnp.zeros_like(stage)
    placed[...] = jnp.zeros_like(placed)
    for sub in range(sub_count):
        count[sub] = 0
    lane = lax.broadcasted_iota(jnp.int32, (at_once, lines, columns), 2)
    slot_lane = lax.broadcasted_iota(jnp.int32, (1, LANES), 1)

    @pl.loop(0, steps)
    def _(step):
        fetch(step).wait()
        for inner in range(depth):
            degree = depth * blk + inner
            begin = first_lane(depth, blk, inner)
            row, offset = begin // LANES, begin % LANES
            end = offset + 2 * degree + 1
            value = arrived[step, :, pl.ds(inner, lines, depth), :]
            value = pltpu.roll(value, (offset + LANES + degree - columns // 2) % LANES, 2)
            here = (lane >= offset) & (lane < end)
            stage[row] = jnp.where(here, value, stage[row])
            stage[row + 1] = jnp.where(lane < end - LANES, value, stage[row + 1])
        for box in range(at_once):
            own = slot[step * at_once + box]
            target = own // total
            rank = count[target]
            count[target] = rank + 1
            out[target, rank // each, :, rank % each] = stage[pl.ds(0, rows), box]
            placed[target] = jnp.where(slot_lane == rank, own % total, placed[target])


def fill_table(tab, diag, cosines, order_ref, factor_ref, before_ref):
    degrees, width, lines, columns = tab.shape
    order = jnp.broadcast_to(order_ref[...], diag.shape)
    next_value = jnp.sqrt(2.0 * order + 3.0) * cosines * diag

    def advance(degree, state):
        previous, before = state
        level = lax.convert_element_type(degree, jnp.float32)
        recur = factor_ref[degree] * (cosines * previous - before * before_ref[degree])
        value = jnp.where(level == order + 1.0, next_value, recur)
        value = jnp.where(level == order, diag, value)
        value = jnp.where(level < order, 0.0, value)
        tab[degree] = jnp.broadcast_to(value[:, None, :], (width, lines, columns))
        return value, previous

    zeros = diag - diag
    lax.fori_loop(0, degrees, advance, (zeros, zeros))


def exchange(
    blocks,
    slots,
    diag,
    cosines,
    orders,
    factor,
    before,
    high,
    low,
    waves,
    quarters,
    source_of,
    placed,
    gathered,
    tab,
    cycles,
    send_far,
    recv_far,
    send_near,
    recv_near,
    send_pair,
    recv_pair,
    send_slot,
    recv_slot,
    local,
    transit,
    send_early,
    recv_early,
    send_far2,
    recv_far2,
    send_back,
    recv_back,
):
    sub_count, groups, _, each, lines, columns = blocks.shape
    degrees, width, _, _ = tab.shape
    parts = diag.shape[0]
    chips = parts // 2
    depth = degrees // parts
    cases = lines // 2
    sizes = [packed_rows(depth, part) for part in range(parts)]
    starts = [sum(sizes[:part]) for part in range(parts)]
    sub = lax.axis_index("sub")
    blk = lax.axis_index("blk")
    chip = blk // 2
    core = blk % 2
    sibling = chip * 2 + (1 - core)

    def start_of(part):
        total = 0
        for before_part in range(parts - 1):
            total = total + jnp.where(part > before_part, sizes[before_part], 0)
        return total

    def sized(part, action):
        rows = packed_rows(depth, part)
        for size in sorted(set(sizes)):
            pl.when(rows == size)(functools.partial(action, size))

    def remote(source, target, send, recv, device):
        return pltpu.make_async_remote_copy(
            src_ref=source,
            dst_ref=target,
            send_sem=send,
            recv_sem=recv,
            device_id=device,
            device_id_type=pl.DeviceIdType.MESH,
        )

    own_rows = start_of(blk)
    feeds = blk == parts - 1 if chips == 2 else None
    forwards = blk == parts - 3 if chips == 2 else None
    heavy, heavy_rows = sizes[-1], starts[-1]

    def early(step, group):
        peer = swapped(sub, step, sub_count)
        return remote(
            blocks.at[peer, group, pl.ds(0, heavy)],
            transit.at[step, group],
            send_early.at[step, group],
            recv_early.at[step, group],
            (sub, parts - 3),
        )

    def far2(step, group):
        peer = swapped(sub, step, sub_count)
        return remote(
            transit.at[step, group],
            gathered.at[sub, group, pl.ds(heavy_rows, heavy)],
            send_far2.at[step, group],
            recv_far2.at[step, group],
            (peer, blk),
        )

    def held(hop, of_core):
        return ((chip + chips - hop) % chips) * 2 + of_core

    def far(step, group, size):
        peer = swapped(sub, step, sub_count)
        return remote(
            blocks.at[peer, group, pl.ds(0, size)],
            gathered.at[sub, group, pl.ds(own_rows, size)],
            send_far.at[step, group],
            recv_far.at[step, group],
            (peer, blk),
        )

    def slot_copy(step):
        peer = swapped(sub, step, sub_count)
        return remote(slots.at[peer], placed.at[sub], send_slot.at[step], recv_slot.at[step], (peer, blk))

    def near(hop, step, group, part, size, own=False):
        source = swapped(sub, step, sub_count)
        rows = pl.ds(start_of(part), size)
        return remote(
            blocks.at[sub, group, pl.ds(0, size)] if own else gathered.at[source, group, rows],
            gathered.at[source, group, rows],
            send_near.at[hop - 1, step, group],
            recv_near.at[hop - 1, step, group],
            (sub, ((chip + hop) % chips) * 2 + core),
        )

    def pair(hop, step, group, part, size, own=False):
        source = swapped(sub, step, sub_count)
        rows = pl.ds(start_of(part), size)
        return remote(
            blocks.at[sub, group, pl.ds(0, size)] if own else gathered.at[source, group, rows],
            gathered.at[source, group, rows],
            send_pair.at[hop, step, group],
            recv_pair.at[hop, step, group],
            (sub, sibling),
        )

    def keep(group, size):
        return pltpu.make_async_copy(
            blocks.at[sub, group, pl.ds(0, size)],
            gathered.at[sub, group, pl.ds(own_rows, size)],
            local.at[group],
        )

    def lean(group):
        return group % 2 == 0

    def direct(group, size):
        return jnp.logical_not(lean(group)) if chips == 2 and size == heavy else group >= 0

    def back(step, group):
        source = swapped(sub, step, sub_count)
        rows = pl.ds(heavy_rows, heavy)
        return remote(
            gathered.at[source, group, rows],
            gathered.at[source, group, rows],
            send_back.at[step, group],
            recv_back.at[step, group],
            (sub, parts - 1),
        )

    barrier = pltpu.get_barrier_semaphore()

    def greet(device):
        pl.semaphore_signal(barrier, inc=1, device_id=device, device_id_type=pl.DeviceIdType.MESH)

    for step in range(1, sub_count):
        greet((swapped(sub, step, sub_count), blk))
    for hop in range(1, chips):
        greet((sub, ((chip + hop) % chips) * 2 + core))
    greet((sub, sibling))
    pl.semaphore_wait(barrier, sub_count - 1 + chips)

    others = sub_count - 1

    def step_at(index):
        return 1 + (index + sub_count // 2 - 1) % others

    for step in range(1, sub_count):
        slot_copy(step).start()
    keep_slot = pltpu.make_async_copy(slots.at[sub], placed.at[sub], local.at[groups])
    keep_slot.start()

    def begin(size):
        @pl.loop(0, groups)
        def _(group):
            @pl.when(direct(group, size))
            def _():
                @pl.loop(0, others)
                def _(index):
                    far(step_at(index), group, size).start()

        @pl.loop(0, groups)
        def _(group):
            for hop in range(1, chips):
                near(hop, 0, group, blk, size, True).start()

            pair(0, 0, group, blk, size, True).start()
            keep(group, size).start()

    sized(blk, begin)
    if chips == 2:

        @pl.when(feeds)
        def _():
            @pl.loop(0, groups)
            def _(group):
                @pl.loop(0, others)
                def _(index):
                    early(step_at(index), group).start()

    fill_table(tab, diag[blk], cosines[blk], orders, factor, before)

    lane = lax.broadcasted_iota(jnp.int32, (each, lines, columns), 2)

    def relay(step, group):
        def act(size):
            @pl.when(direct(group, size))
            def _():
                far(step, group, size).wait_recv()
                if chips != 2:
                    for hop in range(1, chips):
                        near(hop, step, group, blk, size).start()
                elif size != heavy:
                    near(1, step, group, blk, size).start()
                pair(0, step, group, blk, size).start()

        sized(blk, act)

    def forward(step, group):
        @pl.when(forwards)
        def _():
            early(step, group).wait_recv()
            far2(step, group).start()

    def hand_on(step, group):
        for hop in range(1, chips):
            part = held(hop, core)

            def act(size):
                if chips == 2 and size == heavy:

                    @pl.when(step > 0)
                    def _():
                        far2(step, group).wait_recv()

                        @pl.when(lean(group))
                        def _():
                            back(step, group).start()

                    @pl.when(step == 0)
                    def _():
                        near(hop, step, group, part, size).wait_recv()

                else:
                    near(hop, step, group, part, size).wait_recv()
                pair(hop, step, group, part, size).start()

            sized(part, act)
        if chips == 2:

            @pl.when(feeds & (step > 0) & lean(group))
            def _():
                back(step, group).wait_recv()
                pair(0, step, group, blk, heavy).start()

    def finish(step, group):
        for hop in range(chips):
            part = held(hop, 1 - core)
            sized(part, lambda size: pair(hop, step, group, part, size).wait_recv())
        source = swapped(sub, step, sub_count)
        totals = [jnp.zeros((width, lines, columns), jnp.float32) for _ in range(each)]
        for degree in range(degrees):
            part, inner = degree // depth, degree % depth
            begin = first_lane(depth, part, inner)
            row, offset = starts[part] + begin // LANES, begin % LANES
            value = gathered[source, group, row]
            if offset + 2 * degree + 1 > LANES:
                value = jnp.where(lane >= offset, value, gathered[source, group, row + 1])
            shift = (columns // 2 - degree - offset) % LANES
            if shift:
                value = pltpu.roll(value, shift, 2)
            for box in range(each):
                totals[box] = totals[box] + value[box][None] * tab[degree]
        for box in range(each):
            for index in range(width):
                cycles[pl.ds(box * lines * width + index, lines, width), :] = totals[box][index]
        both = cycles[...].reshape(each * cases, 2, width, columns)
        rows = each * cases * width
        both = jnp.concatenate([both[:, 0].reshape(rows, columns), both[:, 1].reshape(rows, columns)], axis=1)
        top = both.astype(jnp.bfloat16)
        rest = (both - top.astype(jnp.float32)).astype(jnp.bfloat16)
        dot = functools.partial(jnp.dot, preferred_element_type=jnp.float32)
        wave = dot(rest, high[...]) + dot(top, low[...]) + dot(top, high[...])
        real, imag = wave[:, :K], wave[:, K:]
        for box in range(each):
            for case in range(cases):
                at = slice((box * cases + case) * width, (box * cases + case + 1) * width)
                waves[source, group, box, case, pl.ds(0, width, 2), :] = real[at]
                waves[source, group, box, case, pl.ds(1, width, 2), :] = imag[at]
                quarters[source, group, box, case, pl.ds(0, width, 2), :] = -imag[at]
                quarters[source, group, box, case, pl.ds(1, width, 2), :] = real[at]

    def waits_keep(size):
        @pl.loop(0, groups)
        def _(group):
            keep(group, size).wait()

    sized(blk, waits_keep)

    chunks = sub_count * groups
    near_lag, pair_lag = 3, 5

    def place_of(chunk):
        later = chunk - groups
        own = chunk < groups
        step = jnp.where(own, 0, step_at(later % others))
        group = jnp.where(own, chunk, later // others)
        return step, group

    @pl.loop(0, chunks + pair_lag)
    def _(chunk):
        @pl.when((chunk >= groups) & (chunk < chunks))
        def _():
            relay(*place_of(chunk))
            if chips == 2:
                forward(*place_of(chunk))

        @pl.when(chunk >= pair_lag)
        def _():
            finish(*place_of(chunk - pair_lag))

        @pl.when((chunk >= near_lag) & (chunk < chunks + near_lag))
        def _():
            hand_on(*place_of(chunk - near_lag))

    def drain(step, group):
        def own_act(size):
            @pl.when((step > 0) & direct(group, size))
            def _():
                far(step, group, size).wait_send()

            if chips == 2 and size == heavy:

                @pl.when(step > 0)
                def _():
                    early(step, group).wait_send()

                @pl.when(step == 0)
                def _():
                    near(1, step, group, blk, size).wait_send()

            else:
                for hop in range(1, chips):
                    near(hop, step, group, blk, size).wait_send()
            pair(0, step, group, blk, size).wait_send()

        sized(blk, own_act)
        if chips == 2:

            @pl.when(forwards & (step > 0))
            def _():
                far2(step, group).wait_send()

                @pl.when(lean(group))
                def _():
                    back(step, group).wait_send()

        for hop in range(1, chips):
            part = held(hop, core)
            sized(part, lambda size: pair(hop, step, group, part, size).wait_send())

    @pl.loop(0, chunks)
    def _(chunk):
        drain(*place_of(chunk))

    for step in range(1, sub_count):
        slot_copy(step).wait()
    keep_slot.wait()
    per_peer = groups * each
    turned = jnp.transpose(placed[:, 0, :])
    where = lax.broadcasted_iota(jnp.int32, (per_peer, LANES), 1)
    rank = lax.broadcasted_iota(jnp.int32, (per_peer, LANES), 0)
    found = jnp.zeros((1, LANES), jnp.int32)
    for source in range(sub_count):
        slot = turned[:per_peer, source : source + 1]
        hit = jnp.where(slot == where, rank + source * per_peer, 0)
        found = found + jnp.sum(hit, axis=0, keepdims=True)
    source_of[...] = found


def phases(source_of, octants, waves, quarters, phase_cos, phase_sin, out, blocks, sems):
    slots, count, cases, places, _, _ = blocks.shape
    boxes = out.shape[0]

    def send(step):
        slot = step % slots
        return pltpu.make_async_copy(blocks.at[slot], out.at[pl.ds(step * count, count)], sems.at[slot])

    @pl.loop(0, boxes // count)
    def _(step):
        slot = step % slots

        @pl.when(step >= slots)
        def _():
            send(step - slots).wait()

        for box in range(count):
            at = step * count + box
            source = source_of[at]
            for place in range(places):
                octant = octants[place, at]
                turn_cos = phase_cos[0, octant]
                turn_sin = phase_sin[0, octant]
                for case in range(cases):
                    blocks[slot, box, case, place] = waves[source, case] * turn_cos + quarters[source, case] * turn_sin
        send(step).start()

    @pl.loop(boxes // count - slots, boxes // count)
    def _(step):
        send(step).wait()


def body(coefficients, owner_slot, child_list):
    boxes, cases, _, depth, columns = coefficients.shape
    sub_count = lax.axis_size("sub")
    parts = lax.axis_size("blk")
    degrees = parts * depth
    width = J // parts
    lines = cases * 2
    per_peer = boxes // sub_count
    each = 2 if per_peer % 2 == 0 else 1
    groups = per_peer // each
    chips = parts // 2
    hops = max(chips - 1, 1)
    rows = max(packed_rows(depth, part) for part in range(parts))
    total_rows = sum(packed_rows(depth, part) for part in range(parts))
    vmem = pl.BlockSpec(memory_space=pltpu.VMEM)
    dma = pltpu.SemaphoreType.DMA
    at_once = 8
    outgoing, slots = pl.pallas_call(
        pack,
        grid_spec=pltpu.PrefetchScalarGridSpec(
            num_scalar_prefetch=1,
            grid=(1,),
            in_specs=[pl.BlockSpec(memory_space=pltpu.HBM)],
            out_specs=(vmem, vmem),
            scratch_shapes=[
                pltpu.VMEM((rows + 1, at_once, lines, columns), jnp.float32),
                pltpu.SMEM((sub_count,), jnp.int32),
                pltpu.VMEM((boxes // at_once, at_once, lines * depth, columns), jnp.float32),
                dma((boxes // at_once,)),
            ],
        ),
        out_shape=(
            jax.ShapeDtypeStruct((sub_count, groups, rows, each, lines, columns), jnp.float32),
            jax.ShapeDtypeStruct((sub_count, 1, LANES), jnp.int32),
        ),
        compiler_params=pltpu.CompilerParams(vmem_limit_bytes=48 * MIB),
        name="pack",
    )(owner_slot, coefficients.reshape(boxes, lines * depth, columns))

    matrix = wave_matrix(degrees, columns, K)
    high = matrix.astype(jnp.bfloat16)
    low = (matrix - high.astype(np.float32)).astype(jnp.bfloat16)
    waves, quarters, source_of = pl.pallas_call(
        exchange,
        out_shape=(
            jax.ShapeDtypeStruct((sub_count, groups, each, cases, 2 * width, K), jnp.float32),
            jax.ShapeDtypeStruct((sub_count, groups, each, cases, 2 * width, K), jnp.float32),
            jax.ShapeDtypeStruct((1, LANES), jnp.int32),
        ),
        in_specs=[vmem] * 9,
        out_specs=(vmem, vmem, vmem),
        scratch_shapes=[
            pltpu.VMEM((sub_count, 1, LANES), jnp.int32),
            pltpu.VMEM((sub_count, groups, total_rows, each, lines, columns), jnp.float32),
            pltpu.VMEM((degrees, width, lines, columns), jnp.float32),
            pltpu.VMEM((each * lines * width, columns), jnp.float32),
            dma((sub_count, groups)),
            dma((sub_count, groups)),
            dma((hops, sub_count, groups)),
            dma((hops, sub_count, groups)),
            dma((chips, sub_count, groups)),
            dma((chips, sub_count, groups)),
            dma((sub_count,)),
            dma((sub_count,)),
            dma((groups + 1,)),
            pltpu.VMEM((sub_count, groups, rows, each, lines, columns) if chips == 2 else (8, LANES), jnp.float32),
            dma((sub_count, groups)),
            dma((sub_count, groups)),
            dma((sub_count, groups)),
            dma((sub_count, groups)),
            dma((sub_count, groups)),
            dma((sub_count, groups)),
        ],
        compiler_params=pltpu.CompilerParams(
            collective_id=0, has_side_effects=True, vmem_limit_bytes=40 * MIB
        ),
        name="exchange",
    )(
        outgoing,
        slots,
        *(jnp.asarray(constant) for constant in legendre_constants(degrees, columns, parts)),
        jnp.asarray(high),
        jnp.asarray(low),
    )

    phase_cos, phase_sin = phase_tables(parts, K)
    blk = lax.axis_index("blk").astype(jnp.int32)
    count = 2 if boxes % 2 == 0 else 1
    slots = min(6, boxes // count)
    own = pl.BlockSpec((1, 8, 2 * width, K), lambda i, source, octants, part: (part[0], 0, 0, 0))
    out = pl.pallas_call(
        lambda source, octants, part, *refs: phases(source, octants, *refs),
        grid_spec=pltpu.PrefetchScalarGridSpec(
            num_scalar_prefetch=3,
            grid=(1,),
            in_specs=[vmem, vmem, own, own],
            out_specs=pl.BlockSpec(memory_space=pltpu.HBM),
            scratch_shapes=[
                pltpu.VMEM((slots, count, cases, 8, 2 * width, K), jnp.float32),
                dma((slots,)),
            ],
        ),
        out_shape=jax.ShapeDtypeStruct((boxes, cases, 8, 2 * width, K), jnp.float32),
        compiler_params=pltpu.CompilerParams(vmem_limit_bytes=32 * MIB),
        name="phases",
    )(
        source_of.reshape(-1),
        child_list.T,
        blk.reshape(1),
        waves.reshape(boxes, cases, 2 * width, K),
        quarters.reshape(boxes, cases, 2 * width, K),
        jnp.asarray(phase_cos),
        jnp.asarray(phase_sin),
    )
    return out.reshape(boxes, cases, 8, width, 2, K)


def solution(mesh):
    placed = (P("sub", None, None, "blk", None), P("sub"), P("sub", None))
    return jax.shard_map(
        body,
        mesh=mesh,
        in_specs=placed,
        out_specs=P("sub", None, None, "blk", None, None),
        check_vma=False,
    )
```

```python
import functools
import math

import jax
import jax.numpy as jnp
import numpy as np
from jax import lax
from jax.experimental import pallas as pl
from jax.experimental.pallas import tpu as pltpu
from jax.sharding import PartitionSpec as P

J = 64
K = 128
LANES = 128
MIB = 1024 * 1024


def ceil_div(value, by):
    return (value + by - 1) // by


def packed_rows(depth, part):
    return ceil_div(depth * depth * (2 * part + 1), LANES)


def first_lane(depth, part, inner):
    return inner * (2 * depth * part) + inner * inner


def swapped(index, step, size):
    total = 0
    bit = 1
    while bit < size:
        total = total + ((index // bit + step // bit) % 2) * bit
        bit *= 2
    return total


def legendre_constants(degrees, columns, parts):
    order = np.abs(np.arange(columns) - degrees).astype(np.float64)
    log_norm = np.array(
        [
            0.5
            * (
                math.log((2 * v + 1) / (4 * math.pi))
                + math.lgamma(2 * v + 1)
                - v * math.log(4.0)
                - 2 * math.lgamma(v + 1)
            )
            for v in order
        ]
    )
    polar = np.pi * (np.arange(J) + 0.5) / J
    diag = np.exp(log_norm[None] + order[None] * np.log(np.sin(polar))[:, None])
    cosines = np.broadcast_to(np.cos(polar)[:, None], (J, columns))
    level = np.arange(degrees, dtype=np.float64)[:, None]
    factor = np.sqrt(np.maximum(4 * level * level - 1, 1.0) / np.maximum(level * level - order[None] ** 2, 1.0))
    before = np.ones_like(factor)
    before[1:] = 1.0 / factor[:-1]
    shape = (parts, J // parts, columns)
    return (
        diag.astype(np.float32).reshape(shape),
        cosines.astype(np.float32).reshape(shape),
        order.astype(np.float32)[None],
        factor.astype(np.float32)[:, None, :],
        before.astype(np.float32)[:, None, :],
    )


def wave_matrix(degrees, columns, azimuths):
    turns = ((np.arange(columns)[:, None] - degrees) * np.arange(azimuths)[None, :]) % azimuths
    angle = 2.0 * np.pi * turns / azimuths
    cosine, sine = np.cos(angle), np.sin(angle)
    upper = np.concatenate([cosine, sine], axis=1)
    lower = np.concatenate([-sine, cosine], axis=1)
    return np.concatenate([upper, lower], axis=0).astype(np.float32)


def phase_tables(parts, azimuths):
    polar = np.pi * (np.arange(J) + 0.5) / J
    azimuth = 2.0 * np.pi * np.arange(azimuths) / azimuths
    octants = np.arange(8)
    sign = [(2 * (octants >> bit & 1) - 1).astype(np.float64)[:, None, None] for bit in range(3)]
    dir_x = np.sin(polar)[:, None] * np.cos(azimuth)[None, :]
    dir_y = np.sin(polar)[:, None] * np.sin(azimuth)[None, :]
    dir_z = np.cos(polar)[:, None] * np.ones_like(azimuth)[None, :]
    phase = 5.5 * (sign[0] * dir_x + sign[1] * dir_y + sign[2] * dir_z)

    def per_part(values):
        twice = np.repeat(values, 2, axis=1).astype(np.float32)
        return twice.reshape(8, parts, 2 * J // parts, azimuths).transpose(1, 0, 2, 3)

    return per_part(np.cos(phase)), per_part(np.sin(phase))


def pack(slots, source, out, placed, stage, count, slot, arrived, sems):
    blk = lax.axis_index("blk")
    _, at_once, depth_lines, columns = arrived.shape
    sub_count, groups, rows, each, lines, _ = out.shape
    depth = depth_lines // lines
    total = sub_count * groups * each
    steps = total // at_once

    def fetch(step):
        return pltpu.make_async_copy(source.at[pl.ds(step * at_once, at_once)], arrived.at[step], sems.at[step])

    fetch_slot = pltpu.make_async_copy(slots, slot, sems.at[steps])
    fetch_slot.start()
    for step in range(steps):
        fetch(step).start()
    stage[...] = jnp.zeros_like(stage)
    placed[...] = jnp.zeros_like(placed)
    for sub in range(sub_count):
        count[sub] = 0
    lane = lax.broadcasted_iota(jnp.int32, (at_once, lines, columns), 2)
    slot_lane = lax.broadcasted_iota(jnp.int32, (1, LANES), 1)
    fetch_slot.wait()

    @pl.loop(0, steps)
    def _(step):
        fetch(step).wait()
        for inner in range(depth):
            degree = depth * blk + inner
            begin = first_lane(depth, blk, inner)
            row, offset = begin // LANES, begin % LANES
            end = offset + 2 * degree + 1
            value = arrived[step, :, pl.ds(inner, lines, depth), :]
            value = pltpu.roll(value, (offset + LANES + degree - columns // 2) % LANES, 2)
            here = (lane >= offset) & (lane < end)
            stage[row] = jnp.where(here, value, stage[row])
            stage[row + 1] = jnp.where(lane < end - LANES, value, stage[row + 1])
        for box in range(at_once):
            own = slot[step * at_once + box]
            target = own // total
            rank = count[target]
            count[target] = rank + 1
            out[target, rank // each, :, rank % each] = stage[pl.ds(0, rows), box]
            placed[target] = jnp.where(slot_lane == rank, own % total, placed[target])


def fill_table(tab, diag, cosines, order_ref, factor_ref, before_ref):
    degrees, width, lines, columns = tab.shape
    order = jnp.broadcast_to(order_ref[...], diag.shape)
    next_value = jnp.sqrt(2.0 * order + 3.0) * cosines * diag

    def advance(degree, state):
        previous, before = state
        level = lax.convert_element_type(degree, jnp.float32)
        recur = factor_ref[degree] * (cosines * previous - before * before_ref[degree])
        value = jnp.where(level == order + 1.0, next_value, recur)
        value = jnp.where(level == order, diag, value)
        value = jnp.where(level < order, 0.0, value)
        tab[degree] = jnp.broadcast_to(value[:, None, :], (width, lines, columns))
        return value, previous

    zeros = diag - diag
    lax.fori_loop(0, degrees, advance, (zeros, zeros))


def exchange(
    blocks,
    slots,
    diag,
    cosines,
    orders,
    factor,
    before,
    high,
    low,
    waves,
    quarters,
    source_of,
    placed,
    gathered,
    tab,
    cycles,
    send_far,
    recv_far,
    send_near,
    recv_near,
    send_pair,
    recv_pair,
    send_slot,
    recv_slot,
    local,
    transit,
    send_early,
    recv_early,
    send_far2,
    recv_far2,
    send_back,
    recv_back,
):
    sub_count, groups, _, each, lines, columns = blocks.shape
    degrees, width, _, _ = tab.shape
    parts = diag.shape[0]
    chips = parts // 2
    depth = degrees // parts
    cases = lines // 2
    sizes = [packed_rows(depth, part) for part in range(parts)]
    starts = [sum(sizes[:part]) for part in range(parts)]
    sub = lax.axis_index("sub")
    blk = lax.axis_index("blk")
    chip = blk // 2
    core = blk % 2
    sibling = chip * 2 + (1 - core)

    def start_of(part):
        total = 0
        for before_part in range(parts - 1):
            total = total + jnp.where(part > before_part, sizes[before_part], 0)
        return total

    def sized(part, action):
        rows = packed_rows(depth, part)
        for size in sorted(set(sizes)):
            pl.when(rows == size)(functools.partial(action, size))

    def remote(source, target, send, recv, device):
        return pltpu.make_async_remote_copy(
            src_ref=source,
            dst_ref=target,
            send_sem=send,
            recv_sem=recv,
            device_id=device,
            device_id_type=pl.DeviceIdType.MESH,
        )

    own_rows = start_of(blk)
    feeds = blk == parts - 1 if chips == 2 else None
    forwards = blk == parts - 3 if chips == 2 else None
    heavy, heavy_rows = sizes[-1], starts[-1]

    def early(step, group):
        peer = swapped(sub, step, sub_count)
        return remote(
            blocks.at[peer, group, pl.ds(0, heavy)],
            transit.at[step, group],
            send_early.at[step, group],
            recv_early.at[step, group],
            (sub, parts - 3),
        )

    def far2(step, group):
        peer = swapped(sub, step, sub_count)
        return remote(
            transit.at[step, group],
            gathered.at[sub, group, pl.ds(heavy_rows, heavy)],
            send_far2.at[step, group],
            recv_far2.at[step, group],
            (peer, blk),
        )

    def held(hop, of_core):
        return ((chip + chips - hop) % chips) * 2 + of_core

    def far(step, group, size):
        peer = swapped(sub, step, sub_count)
        return remote(
            blocks.at[peer, group, pl.ds(0, size)],
            gathered.at[sub, group, pl.ds(own_rows, size)],
            send_far.at[step, group],
            recv_far.at[step, group],
            (peer, blk),
        )

    def slot_copy(step):
        peer = swapped(sub, step, sub_count)
        return remote(slots.at[peer], placed.at[sub], send_slot.at[step], recv_slot.at[step], (peer, blk))

    def near(hop, step, group, part, size, own=False):
        source = swapped(sub, step, sub_count)
        rows = pl.ds(start_of(part), size)
        return remote(
            blocks.at[sub, group, pl.ds(0, size)] if own else gathered.at[source, group, rows],
            gathered.at[source, group, rows],
            send_near.at[hop - 1, step, group],
            recv_near.at[hop - 1, step, group],
            (sub, ((chip + hop) % chips) * 2 + core),
        )

    def pair(hop, step, group, part, size, own=False):
        source = swapped(sub, step, sub_count)
        rows = pl.ds(start_of(part), size)
        return remote(
            blocks.at[sub, group, pl.ds(0, size)] if own else gathered.at[source, group, rows],
            gathered.at[source, group, rows],
            send_pair.at[hop, step, group],
            recv_pair.at[hop, step, group],
            (sub, sibling),
        )

    def keep(group, size):
        return pltpu.make_async_copy(
            blocks.at[sub, group, pl.ds(0, size)],
            gathered.at[sub, group, pl.ds(own_rows, size)],
            local.at[group],
        )

    def lean(group):
        return group % 2 == 0

    def direct(group, size):
        return jnp.logical_not(lean(group)) if chips == 2 and size == heavy else group >= 0

    def back(step, group):
        source = swapped(sub, step, sub_count)
        rows = pl.ds(heavy_rows, heavy)
        return remote(
            gathered.at[source, group, rows],
            gathered.at[source, group, rows],
            send_back.at[step, group],
            recv_back.at[step, group],
            (sub, parts - 1),
        )

    barrier = pltpu.get_barrier_semaphore()

    def greet(device):
        pl.semaphore_signal(barrier, inc=1, device_id=device, device_id_type=pl.DeviceIdType.MESH)

    for step in range(1, sub_count):
        greet((swapped(sub, step, sub_count), blk))
    for hop in range(1, chips):
        greet((sub, ((chip + hop) % chips) * 2 + core))
    greet((sub, sibling))
    pl.semaphore_wait(barrier, sub_count - 1 + chips)

    others = sub_count - 1

    def step_at(index):
        return 1 + (index + sub_count // 2 - 1) % others

    for step in range(1, sub_count):
        slot_copy(step).start()
    keep_slot = pltpu.make_async_copy(slots.at[sub], placed.at[sub], local.at[groups])
    keep_slot.start()

    def begin(size):
        @pl.loop(0, groups)
        def _(group):
            @pl.when(direct(group, size))
            def _():
                @pl.loop(0, others)
                def _(index):
                    far(step_at(index), group, size).start()

        @pl.loop(0, groups)
        def _(group):
            for hop in range(1, chips):
                near(hop, 0, group, blk, size, True).start()

            pair(0, 0, group, blk, size, True).start()
            keep(group, size).start()

    sized(blk, begin)
    if chips == 2:

        @pl.when(feeds)
        def _():
            @pl.loop(0, groups)
            def _(group):
                @pl.loop(0, others)
                def _(index):
                    early(step_at(index), group).start()

    fill_table(tab, diag[blk], cosines[blk], orders, factor, before)

    lane = lax.broadcasted_iota(jnp.int32, (each, lines, columns), 2)

    def relay(step, group):
        def act(size):
            @pl.when(direct(group, size))
            def _():
                far(step, group, size).wait_recv()
                if chips != 2:
                    for hop in range(1, chips):
                        near(hop, step, group, blk, size).start()
                elif size != heavy:
                    near(1, step, group, blk, size).start()
                pair(0, step, group, blk, size).start()

        sized(blk, act)

    def forward(step, group):
        @pl.when(forwards)
        def _():
            early(step, group).wait_recv()
            far2(step, group).start()

    def hand_on(step, group):
        for hop in range(1, chips):
            part = held(hop, core)

            def act(size):
                if chips == 2 and size == heavy:

                    @pl.when(step > 0)
                    def _():
                        far2(step, group).wait_recv()

                        @pl.when(lean(group))
                        def _():
                            back(step, group).start()

                    @pl.when(step == 0)
                    def _():
                        near(hop, step, group, part, size).wait_recv()

                else:
                    near(hop, step, group, part, size).wait_recv()
                pair(hop, step, group, part, size).start()

            sized(part, act)
        if chips == 2:

            @pl.when(feeds & (step > 0) & lean(group))
            def _():
                back(step, group).wait_recv()
                pair(0, step, group, blk, heavy).start()

    def finish(step, group):
        for hop in range(chips):
            part = held(hop, 1 - core)
            sized(part, lambda size: pair(hop, step, group, part, size).wait_recv())
        source = swapped(sub, step, sub_count)
        totals = [jnp.zeros((width, lines, columns), jnp.float32) for _ in range(each)]
        for degree in range(degrees):
            part, inner = degree // depth, degree % depth
            begin = first_lane(depth, part, inner)
            row, offset = starts[part] + begin // LANES, begin % LANES
            value = gathered[source, group, row]
            if offset + 2 * degree + 1 > LANES:
                value = jnp.where(lane >= offset, value, gathered[source, group, row + 1])
            shift = (columns // 2 - degree - offset) % LANES
            if shift:
                value = pltpu.roll(value, shift, 2)
            for box in range(each):
                totals[box] = totals[box] + value[box][None] * tab[degree]
        for box in range(each):
            for index in range(width):
                cycles[pl.ds(box * lines * width + index, lines, width), :] = totals[box][index]
        both = cycles[...].reshape(each * cases, 2, width, columns)
        rows = each * cases * width
        both = jnp.concatenate([both[:, 0].reshape(rows, columns), both[:, 1].reshape(rows, columns)], axis=1)
        top = both.astype(jnp.bfloat16)
        rest = (both - top.astype(jnp.float32)).astype(jnp.bfloat16)
        dot = functools.partial(jnp.dot, preferred_element_type=jnp.float32)
        wave = dot(rest, high[...]) + dot(top, low[...]) + dot(top, high[...])
        real, imag = wave[:, :K], wave[:, K:]
        for box in range(each):
            for case in range(cases):
                at = slice((box * cases + case) * width, (box * cases + case + 1) * width)
                waves[source, group, box, case, pl.ds(0, width, 2), :] = real[at]
                waves[source, group, box, case, pl.ds(1, width, 2), :] = imag[at]
                quarters[source, group, box, case, pl.ds(0, width, 2), :] = -imag[at]
                quarters[source, group, box, case, pl.ds(1, width, 2), :] = real[at]

    def waits_keep(size):
        @pl.loop(0, groups)
        def _(group):
            keep(group, size).wait()

    sized(blk, waits_keep)

    chunks = sub_count * groups
    near_lag, pair_lag = 5, 7

    def place_of(chunk):
        later = chunk - groups
        own = chunk < groups
        step = jnp.where(own, 0, step_at(later % others))
        group = jnp.where(own, chunk, later // others)
        return step, group

    @pl.loop(0, chunks + pair_lag)
    def _(chunk):
        @pl.when((chunk >= groups) & (chunk < chunks))
        def _():
            relay(*place_of(chunk))
            if chips == 2:
                forward(*place_of(chunk))

        @pl.when(chunk >= pair_lag)
        def _():
            finish(*place_of(chunk - pair_lag))

        @pl.when((chunk >= near_lag) & (chunk < chunks + near_lag))
        def _():
            hand_on(*place_of(chunk - near_lag))

    def drain(step, group):
        def own_act(size):
            @pl.when((step > 0) & direct(group, size))
            def _():
                far(step, group, size).wait_send()

            if chips == 2 and size == heavy:

                @pl.when(step > 0)
                def _():
                    early(step, group).wait_send()

                @pl.when(step == 0)
                def _():
                    near(1, step, group, blk, size).wait_send()

            else:
                for hop in range(1, chips):
                    near(hop, step, group, blk, size).wait_send()
            pair(0, step, group, blk, size).wait_send()

        sized(blk, own_act)
        if chips == 2:

            @pl.when(forwards & (step > 0))
            def _():
                far2(step, group).wait_send()

                @pl.when(lean(group))
                def _():
                    back(step, group).wait_send()

        for hop in range(1, chips):
            part = held(hop, core)
            sized(part, lambda size: pair(hop, step, group, part, size).wait_send())

    @pl.loop(0, chunks)
    def _(chunk):
        drain(*place_of(chunk))

    for step in range(1, sub_count):
        slot_copy(step).wait()
    keep_slot.wait()
    per_peer = groups * each
    turned = jnp.transpose(placed[:, 0, :])
    where = lax.broadcasted_iota(jnp.int32, (per_peer, LANES), 1)
    rank = lax.broadcasted_iota(jnp.int32, (per_peer, LANES), 0)
    found = jnp.zeros((1, LANES), jnp.int32)
    for source in range(sub_count):
        slot = turned[:per_peer, source : source + 1]
        hit = jnp.where(slot == where, rank + source * per_peer, 0)
        found = found + jnp.sum(hit, axis=0, keepdims=True)
    source_of[...] = found


def phases(source_of, octants, waves, quarters, phase_cos, phase_sin, out, blocks, sems):
    slots, count, cases, places, _, _ = blocks.shape
    boxes = out.shape[0]

    def send(step):
        slot = step % slots
        return pltpu.make_async_copy(blocks.at[slot], out.at[pl.ds(step * count, count)], sems.at[slot])

    @pl.loop(0, boxes // count)
    def _(step):
        slot = step % slots

        @pl.when(step >= slots)
        def _():
            send(step - slots).wait()

        for box in range(count):
            at = step * count + box
            source = source_of[at]
            for place in range(places):
                octant = octants[place, at]
                turn_cos = phase_cos[0, octant]
                turn_sin = phase_sin[0, octant]
                for case in range(cases):
                    blocks[slot, box, case, place] = waves[source, case] * turn_cos + quarters[source, case] * turn_sin
        send(step).start()

    @pl.loop(boxes // count - slots, boxes // count)
    def _(step):
        send(step).wait()


def body(coefficients, owner_slot, child_list):
    boxes, cases, _, depth, columns = coefficients.shape
    sub_count = lax.axis_size("sub")
    parts = lax.axis_size("blk")
    degrees = parts * depth
    width = J // parts
    lines = cases * 2
    per_peer = boxes // sub_count
    each = 2 if per_peer % 2 == 0 else 1
    groups = per_peer // each
    chips = parts // 2
    hops = max(chips - 1, 1)
    rows = max(packed_rows(depth, part) for part in range(parts))
    total_rows = sum(packed_rows(depth, part) for part in range(parts))
    vmem = pl.BlockSpec(memory_space=pltpu.VMEM)
    dma = pltpu.SemaphoreType.DMA
    at_once = 8
    outgoing, slots = pl.pallas_call(
        pack,
        in_specs=[pl.BlockSpec(memory_space=pltpu.HBM)] * 2,
        out_specs=(vmem, vmem),
        scratch_shapes=[
            pltpu.VMEM((rows + 1, at_once, lines, columns), jnp.float32),
            pltpu.SMEM((sub_count,), jnp.int32),
            pltpu.SMEM((boxes,), jnp.int32),
            pltpu.VMEM((boxes // at_once, at_once, lines * depth, columns), jnp.float32),
            dma((boxes // at_once + 1,)),
        ],
        out_shape=(
            jax.ShapeDtypeStruct((sub_count, groups, rows, each, lines, columns), jnp.float32),
            jax.ShapeDtypeStruct((sub_count, 1, LANES), jnp.int32),
        ),
        compiler_params=pltpu.CompilerParams(vmem_limit_bytes=48 * MIB),
        name="pack",
    )(owner_slot, coefficients.reshape(boxes, lines * depth, columns))

    matrix = wave_matrix(degrees, columns, K)
    high = matrix.astype(jnp.bfloat16)
    low = (matrix - high.astype(np.float32)).astype(jnp.bfloat16)
    waves, quarters, source_of = pl.pallas_call(
        exchange,
        out_shape=(
            jax.ShapeDtypeStruct((sub_count, groups, each, cases, 2 * width, K), jnp.float32),
            jax.ShapeDtypeStruct((sub_count, groups, each, cases, 2 * width, K), jnp.float32),
            jax.ShapeDtypeStruct((1, LANES), jnp.int32),
        ),
        in_specs=[vmem] * 9,
        out_specs=(vmem, vmem, vmem),
        scratch_shapes=[
            pltpu.VMEM((sub_count, 1, LANES), jnp.int32),
            pltpu.VMEM((sub_count, groups, total_rows, each, lines, columns), jnp.float32),
            pltpu.VMEM((degrees, width, lines, columns), jnp.float32),
            pltpu.VMEM((each * lines * width, columns), jnp.float32),
            dma((sub_count, groups)),
            dma((sub_count, groups)),
            dma((hops, sub_count, groups)),
            dma((hops, sub_count, groups)),
            dma((chips, sub_count, groups)),
            dma((chips, sub_count, groups)),
            dma((sub_count,)),
            dma((sub_count,)),
            dma((groups + 1,)),
            pltpu.VMEM((sub_count, groups, rows, each, lines, columns) if chips == 2 else (8, LANES), jnp.float32),
            dma((sub_count, groups)),
            dma((sub_count, groups)),
            dma((sub_count, groups)),
            dma((sub_count, groups)),
            dma((sub_count, groups)),
            dma((sub_count, groups)),
        ],
        compiler_params=pltpu.CompilerParams(
            collective_id=0, has_side_effects=True, vmem_limit_bytes=40 * MIB
        ),
        name="exchange",
    )(
        outgoing,
        slots,
        *(jnp.asarray(constant) for constant in legendre_constants(degrees, columns, parts)),
        jnp.asarray(high),
        jnp.asarray(low),
    )

    phase_cos, phase_sin = phase_tables(parts, K)
    blk = lax.axis_index("blk").astype(jnp.int32)
    count = 2 if boxes % 2 == 0 else 1
    slots = min(6, boxes // count)
    own = pl.BlockSpec((1, 8, 2 * width, K), lambda i, source, octants, part: (part[0], 0, 0, 0))
    out = pl.pallas_call(
        lambda source, octants, part, *refs: phases(source, octants, *refs),
        grid_spec=pltpu.PrefetchScalarGridSpec(
            num_scalar_prefetch=3,
            grid=(1,),
            in_specs=[vmem, vmem, own, own],
            out_specs=pl.BlockSpec(memory_space=pltpu.HBM),
            scratch_shapes=[
                pltpu.VMEM((slots, count, cases, 8, 2 * width, K), jnp.float32),
                dma((slots,)),
            ],
        ),
        out_shape=jax.ShapeDtypeStruct((boxes, cases, 8, 2 * width, K), jnp.float32),
        compiler_params=pltpu.CompilerParams(vmem_limit_bytes=32 * MIB),
        name="phases",
    )(
        source_of.reshape(-1),
        child_list.T,
        blk.reshape(1),
        waves.reshape(boxes, cases, 2 * width, K),
        quarters.reshape(boxes, cases, 2 * width, K),
        jnp.asarray(phase_cos),
        jnp.asarray(phase_sin),
    )
    return out.reshape(boxes, cases, 8, width, 2, K)


def solution(mesh):
    placed = (P("sub", None, None, "blk", None), P("sub"), P("sub", None))
    return jax.shard_map(
        body,
        mesh=mesh,
        in_specs=placed,
        out_specs=P("sub", None, None, "blk", None, None),
        check_vma=False,
    )
```

```python
import functools
import math

import jax
import jax.numpy as jnp
import numpy as np
from jax import lax
from jax.experimental import pallas as pl
from jax.experimental.pallas import tpu as pltpu
from jax.sharding import PartitionSpec as P

J = 64
K = 128
LANES = 128
MIB = 1024 * 1024


def ceil_div(value, by):
    return (value + by - 1) // by


def packed_rows(depth, part):
    return ceil_div(depth * depth * (2 * part + 1), LANES)


def first_lane(depth, part, inner):
    return inner * (2 * depth * part) + inner * inner


def swapped(index, step, size):
    total = 0
    bit = 1
    while bit < size:
        total = total + ((index // bit + step // bit) % 2) * bit
        bit *= 2
    return total


def legendre_constants(degrees, columns, parts):
    order = np.abs(np.arange(columns) - degrees).astype(np.float64)
    log_norm = np.array(
        [
            0.5
            * (
                math.log((2 * v + 1) / (4 * math.pi))
                + math.lgamma(2 * v + 1)
                - v * math.log(4.0)
                - 2 * math.lgamma(v + 1)
            )
            for v in order
        ]
    )
    polar = np.pi * (np.arange(J) + 0.5) / J
    diag = np.exp(log_norm[None] + order[None] * np.log(np.sin(polar))[:, None])
    cosines = np.broadcast_to(np.cos(polar)[:, None], (J, columns))
    level = np.arange(degrees, dtype=np.float64)[:, None]
    factor = np.sqrt(np.maximum(4 * level * level - 1, 1.0) / np.maximum(level * level - order[None] ** 2, 1.0))
    before = np.ones_like(factor)
    before[1:] = 1.0 / factor[:-1]
    shape = (parts, J // parts, columns)
    return (
        diag.astype(np.float32).reshape(shape),
        cosines.astype(np.float32).reshape(shape),
        order.astype(np.float32)[None],
        factor.astype(np.float32)[:, None, :],
        before.astype(np.float32)[:, None, :],
    )


def wave_matrix(degrees, columns, azimuths):
    turns = ((np.arange(columns)[:, None] - degrees) * np.arange(azimuths)[None, :]) % azimuths
    angle = 2.0 * np.pi * turns / azimuths
    cosine, sine = np.cos(angle), np.sin(angle)
    upper = np.concatenate([cosine, sine], axis=1)
    lower = np.concatenate([-sine, cosine], axis=1)
    return np.concatenate([upper, lower], axis=0).astype(np.float32)


def phase_tables(parts, azimuths):
    polar = np.pi * (np.arange(J) + 0.5) / J
    azimuth = 2.0 * np.pi * np.arange(azimuths) / azimuths
    octants = np.arange(8)
    sign = [(2 * (octants >> bit & 1) - 1).astype(np.float64)[:, None, None] for bit in range(3)]
    dir_x = np.sin(polar)[:, None] * np.cos(azimuth)[None, :]
    dir_y = np.sin(polar)[:, None] * np.sin(azimuth)[None, :]
    dir_z = np.cos(polar)[:, None] * np.ones_like(azimuth)[None, :]
    phase = 5.5 * (sign[0] * dir_x + sign[1] * dir_y + sign[2] * dir_z)

    def per_part(values):
        twice = np.repeat(values, 2, axis=1).astype(np.float32)
        return twice.reshape(8, parts, 2 * J // parts, azimuths).transpose(1, 0, 2, 3)

    return per_part(np.cos(phase)), per_part(np.sin(phase))


def pack(slots, source, out, placed, stage, count, slot, arrived, sems):
    blk = lax.axis_index("blk")
    _, at_once, depth_lines, columns = arrived.shape
    sub_count, groups, rows, each, lines, _ = out.shape
    depth = depth_lines // lines
    total = sub_count * groups * each
    steps = total // at_once

    def fetch(step):
        return pltpu.make_async_copy(source.at[pl.ds(step * at_once, at_once)], arrived.at[step], sems.at[step])

    fetch_slot = pltpu.make_async_copy(slots, slot, sems.at[steps])
    fetch_slot.start()
    for step in range(steps):
        fetch(step).start()
    stage[...] = jnp.zeros_like(stage)
    placed[...] = jnp.zeros_like(placed)
    for sub in range(sub_count):
        count[sub] = 0
    lane = lax.broadcasted_iota(jnp.int32, (at_once, lines, columns), 2)
    slot_lane = lax.broadcasted_iota(jnp.int32, (1, LANES), 1)
    fetch_slot.wait()

    @pl.loop(0, steps)
    def _(step):
        fetch(step).wait()
        for inner in range(depth):
            degree = depth * blk + inner
            begin = first_lane(depth, blk, inner)
            row, offset = begin // LANES, begin % LANES
            end = offset + 2 * degree + 1
            value = arrived[step, :, pl.ds(inner, lines, depth), :]
            value = pltpu.roll(value, (offset + LANES + degree - columns // 2) % LANES, 2)
            here = (lane >= offset) & (lane < end)
            pltpu.store(stage.at[row], value, mask=here)
            pltpu.store(stage.at[row + 1], value, mask=lane < end - LANES)
        for box in range(at_once):
            own = slot[step * at_once + box]
            target = own // total
            rank = count[target]
            count[target] = rank + 1
            out[target, rank // each, :, rank % each] = stage[pl.ds(0, rows), box]
            placed[target] = jnp.where(slot_lane == rank, own % total, placed[target])


def fill_table(tab, diag, cosines, order_ref, factor_ref, before_ref):
    degrees, width, lines, columns = tab.shape
    order = jnp.broadcast_to(order_ref[...], diag.shape)
    next_value = jnp.sqrt(2.0 * order + 3.0) * cosines * diag

    def advance(degree, state):
        previous, before = state
        level = lax.convert_element_type(degree, jnp.float32)
        recur = factor_ref[degree] * (cosines * previous - before * before_ref[degree])
        value = jnp.where(level == order + 1.0, next_value, recur)
        value = jnp.where(level == order, diag, value)
        value = jnp.where(level < order, 0.0, value)
        tab[degree] = jnp.broadcast_to(value[:, None, :], (width, lines, columns))
        return value, previous

    zeros = diag - diag
    lax.fori_loop(0, degrees, advance, (zeros, zeros))


def exchange(
    blocks,
    slots,
    diag,
    cosines,
    orders,
    factor,
    before,
    high,
    low,
    waves,
    quarters,
    source_of,
    placed,
    gathered,
    tab,
    cycles,
    send_far,
    recv_far,
    send_near,
    recv_near,
    send_pair,
    recv_pair,
    send_slot,
    recv_slot,
    local,
    transit,
    send_early,
    recv_early,
    send_far2,
    recv_far2,
    send_back,
    recv_back,
):
    sub_count, groups, _, each, lines, columns = blocks.shape
    degrees, width, _, _ = tab.shape
    parts = diag.shape[0]
    chips = parts // 2
    depth = degrees // parts
    cases = lines // 2
    sizes = [packed_rows(depth, part) for part in range(parts)]
    starts = [sum(sizes[:part]) for part in range(parts)]
    sub = lax.axis_index("sub")
    blk = lax.axis_index("blk")
    chip = blk // 2
    core = blk % 2
    sibling = chip * 2 + (1 - core)

    def start_of(part):
        total = 0
        for before_part in range(parts - 1):
            total = total + jnp.where(part > before_part, sizes[before_part], 0)
        return total

    def sized(part, action):
        rows = packed_rows(depth, part)
        for size in sorted(set(sizes)):
            pl.when(rows == size)(functools.partial(action, size))

    def remote(source, target, send, recv, device):
        return pltpu.make_async_remote_copy(
            src_ref=source,
            dst_ref=target,
            send_sem=send,
            recv_sem=recv,
            device_id=device,
            device_id_type=pl.DeviceIdType.MESH,
        )

    own_rows = start_of(blk)
    feeds = blk == parts - 1 if chips == 2 else None
    forwards = blk == parts - 3 if chips == 2 else None
    heavy, heavy_rows = sizes[-1], starts[-1]

    def early(step, group):
        peer = swapped(sub, step, sub_count)
        return remote(
            blocks.at[peer, group, pl.ds(0, heavy)],
            transit.at[step, group],
            send_early.at[step, group],
            recv_early.at[step, group],
            (sub, parts - 3),
        )

    def far2(step, group):
        peer = swapped(sub, step, sub_count)
        return remote(
            transit.at[step, group],
            gathered.at[sub, group, pl.ds(heavy_rows, heavy)],
            send_far2.at[step, group],
            recv_far2.at[step, group],
            (peer, blk),
        )

    def held(hop, of_core):
        return ((chip + chips - hop) % chips) * 2 + of_core

    def far(step, group, size):
        peer = swapped(sub, step, sub_count)
        return remote(
            blocks.at[peer, group, pl.ds(0, size)],
            gathered.at[sub, group, pl.ds(own_rows, size)],
            send_far.at[step, group],
            recv_far.at[step, group],
            (peer, blk),
        )

    def slot_copy(step):
        peer = swapped(sub, step, sub_count)
        return remote(slots.at[peer], placed.at[sub], send_slot.at[step], recv_slot.at[step], (peer, blk))

    def near(hop, step, group, part, size, own=False):
        source = swapped(sub, step, sub_count)
        rows = pl.ds(start_of(part), size)
        return remote(
            blocks.at[sub, group, pl.ds(0, size)] if own else gathered.at[source, group, rows],
            gathered.at[source, group, rows],
            send_near.at[hop - 1, step, group],
            recv_near.at[hop - 1, step, group],
            (sub, ((chip + hop) % chips) * 2 + core),
        )

    def pair(hop, step, group, part, size, own=False):
        source = swapped(sub, step, sub_count)
        rows = pl.ds(start_of(part), size)
        return remote(
            blocks.at[sub, group, pl.ds(0, size)] if own else gathered.at[source, group, rows],
            gathered.at[source, group, rows],
            send_pair.at[hop, step, group],
            recv_pair.at[hop, step, group],
            (sub, sibling),
        )

    def keep(group, size):
        return pltpu.make_async_copy(
            blocks.at[sub, group, pl.ds(0, size)],
            gathered.at[sub, group, pl.ds(own_rows, size)],
            local.at[group],
        )

    def lean(group):
        return group % 2 == 0

    def direct(group, size):
        return jnp.logical_not(lean(group)) if chips == 2 and size == heavy else group >= 0

    def back(step, group):
        source = swapped(sub, step, sub_count)
        rows = pl.ds(heavy_rows, heavy)
        return remote(
            gathered.at[source, group, rows],
            gathered.at[source, group, rows],
            send_back.at[step, group],
            recv_back.at[step, group],
            (sub, parts - 1),
        )

    barrier = pltpu.get_barrier_semaphore()

    def greet(device):
        pl.semaphore_signal(barrier, inc=1, device_id=device, device_id_type=pl.DeviceIdType.MESH)

    for step in range(1, sub_count):
        greet((swapped(sub, step, sub_count), blk))
    for hop in range(1, chips):
        greet((sub, ((chip + hop) % chips) * 2 + core))
    greet((sub, sibling))
    pl.semaphore_wait(barrier, sub_count - 1 + chips)

    others = sub_count - 1

    def step_at(index):
        return 1 + (index + sub_count // 2 - 1) % others

    for step in range(1, sub_count):
        slot_copy(step).start()
    keep_slot = pltpu.make_async_copy(slots.at[sub], placed.at[sub], local.at[groups])
    keep_slot.start()

    def begin(size):
        @pl.loop(0, groups)
        def _(group):
            @pl.when(direct(group, size))
            def _():
                @pl.loop(0, others)
                def _(index):
                    far(step_at(index), group, size).start()

        @pl.loop(0, groups)
        def _(group):
            for hop in range(1, chips):
                near(hop, 0, group, blk, size, True).start()

            pair(0, 0, group, blk, size, True).start()
            keep(group, size).start()

    sized(blk, begin)
    if chips == 2:

        @pl.when(feeds)
        def _():
            @pl.loop(0, groups)
            def _(group):
                @pl.loop(0, others)
                def _(index):
                    early(step_at(index), group).start()

    fill_table(tab, diag[blk], cosines[blk], orders, factor, before)

    lane = lax.broadcasted_iota(jnp.int32, (each, lines, columns), 2)

    def relay(step, group):
        def act(size):
            @pl.when(direct(group, size))
            def _():
                far(step, group, size).wait_recv()
                if chips != 2:
                    for hop in range(1, chips):
                        near(hop, step, group, blk, size).start()
                elif size != heavy:
                    near(1, step, group, blk, size).start()
                pair(0, step, group, blk, size).start()

        sized(blk, act)

    def forward(step, group):
        @pl.when(forwards)
        def _():
            early(step, group).wait_recv()
            far2(step, group).start()

    def hand_on(step, group):
        for hop in range(1, chips):
            part = held(hop, core)

            def act(size):
                if chips == 2 and size == heavy:

                    @pl.when(step > 0)
                    def _():
                        far2(step, group).wait_recv()

                        @pl.when(lean(group))
                        def _():
                            back(step, group).start()

                    @pl.when(step == 0)
                    def _():
                        near(hop, step, group, part, size).wait_recv()

                else:
                    near(hop, step, group, part, size).wait_recv()
                pair(hop, step, group, part, size).start()

            sized(part, act)
        if chips == 2:

            @pl.when(feeds & (step > 0) & lean(group))
            def _():
                back(step, group).wait_recv()
                pair(0, step, group, blk, heavy).start()

    def finish(step, group):
        for hop in range(chips):
            part = held(hop, 1 - core)
            sized(part, lambda size: pair(hop, step, group, part, size).wait_recv())
        source = swapped(sub, step, sub_count)
        totals = [jnp.zeros((width, lines, columns), jnp.float32) for _ in range(each)]
        for degree in range(degrees):
            part, inner = degree // depth, degree % depth
            begin = first_lane(depth, part, inner)
            row, offset = starts[part] + begin // LANES, begin % LANES
            value = gathered[source, group, row]
            if offset + 2 * degree + 1 > LANES:
                value = jnp.where(lane >= offset, value, gathered[source, group, row + 1])
            shift = (columns // 2 - degree - offset) % LANES
            if shift:
                value = pltpu.roll(value, shift, 2)
            for box in range(each):
                totals[box] = totals[box] + value[box][None] * tab[degree]
        for box in range(each):
            for index in range(width):
                cycles[pl.ds(box * lines * width + index, lines, width), :] = totals[box][index]
        both = cycles[...].reshape(each * cases, 2, width, columns)
        rows = each * cases * width
        both = jnp.concatenate([both[:, 0].reshape(rows, columns), both[:, 1].reshape(rows, columns)], axis=1)
        top = both.astype(jnp.bfloat16)
        rest = (both - top.astype(jnp.float32)).astype(jnp.bfloat16)
        dot = functools.partial(jnp.dot, preferred_element_type=jnp.float32)
        wave = dot(rest, high[...]) + dot(top, low[...]) + dot(top, high[...])
        real, imag = wave[:, :K], wave[:, K:]
        for box in range(each):
            for case in range(cases):
                at = slice((box * cases + case) * width, (box * cases + case + 1) * width)
                waves[source, group, box, case, pl.ds(0, width, 2), :] = real[at]
                waves[source, group, box, case, pl.ds(1, width, 2), :] = imag[at]
                quarters[source, group, box, case, pl.ds(0, width, 2), :] = -imag[at]
                quarters[source, group, box, case, pl.ds(1, width, 2), :] = real[at]

    def waits_keep(size):
        @pl.loop(0, groups)
        def _(group):
            keep(group, size).wait()

    sized(blk, waits_keep)

    chunks = sub_count * groups
    near_lag, pair_lag = 5, 7

    def place_of(chunk):
        later = chunk - groups
        own = chunk < groups
        step = jnp.where(own, 0, step_at(later % others))
        group = jnp.where(own, chunk, later // others)
        return step, group

    @pl.loop(0, chunks + pair_lag)
    def _(chunk):
        @pl.when((chunk >= groups) & (chunk < chunks))
        def _():
            relay(*place_of(chunk))
            if chips == 2:
                forward(*place_of(chunk))

        @pl.when(chunk >= pair_lag)
        def _():
            finish(*place_of(chunk - pair_lag))

        @pl.when((chunk >= near_lag) & (chunk < chunks + near_lag))
        def _():
            hand_on(*place_of(chunk - near_lag))

    def drain(step, group):
        def own_act(size):
            @pl.when((step > 0) & direct(group, size))
            def _():
                far(step, group, size).wait_send()

            if chips == 2 and size == heavy:

                @pl.when(step > 0)
                def _():
                    early(step, group).wait_send()

                @pl.when(step == 0)
                def _():
                    near(1, step, group, blk, size).wait_send()

            else:
                for hop in range(1, chips):
                    near(hop, step, group, blk, size).wait_send()
            pair(0, step, group, blk, size).wait_send()

        sized(blk, own_act)
        if chips == 2:

            @pl.when(forwards & (step > 0))
            def _():
                far2(step, group).wait_send()

                @pl.when(lean(group))
                def _():
                    back(step, group).wait_send()

        for hop in range(1, chips):
            part = held(hop, core)
            sized(part, lambda size: pair(hop, step, group, part, size).wait_send())

    @pl.loop(0, chunks)
    def _(chunk):
        drain(*place_of(chunk))

    for step in range(1, sub_count):
        slot_copy(step).wait()
    keep_slot.wait()
    per_peer = groups * each
    turned = jnp.transpose(placed[:, 0, :])
    where = lax.broadcasted_iota(jnp.int32, (per_peer, LANES), 1)
    rank = lax.broadcasted_iota(jnp.int32, (per_peer, LANES), 0)
    found = jnp.zeros((1, LANES), jnp.int32)
    for source in range(sub_count):
        slot = turned[:per_peer, source : source + 1]
        hit = jnp.where(slot == where, rank + source * per_peer, 0)
        found = found + jnp.sum(hit, axis=0, keepdims=True)
    source_of[...] = found


def phases(source_of, octants, waves, quarters, phase_cos, phase_sin, out, blocks, sems):
    slots, count, cases, places, _, _ = blocks.shape
    boxes = out.shape[0]

    def send(step):
        slot = step % slots
        return pltpu.make_async_copy(blocks.at[slot], out.at[pl.ds(step * count, count)], sems.at[slot])

    @pl.loop(0, boxes // count)
    def _(step):
        slot = step % slots

        @pl.when(step >= slots)
        def _():
            send(step - slots).wait()

        for box in range(count):
            at = step * count + box
            source = source_of[at]
            for place in range(places):
                octant = octants[place, at]
                turn_cos = phase_cos[0, octant]
                turn_sin = phase_sin[0, octant]
                for case in range(cases):
                    blocks[slot, box, case, place] = waves[source, case] * turn_cos + quarters[source, case] * turn_sin
        send(step).start()

    @pl.loop(boxes // count - slots, boxes // count)
    def _(step):
        send(step).wait()


def body(coefficients, owner_slot, child_list):
    boxes, cases, _, depth, columns = coefficients.shape
    sub_count = lax.axis_size("sub")
    parts = lax.axis_size("blk")
    degrees = parts * depth
    width = J // parts
    lines = cases * 2
    per_peer = boxes // sub_count
    each = 2 if per_peer % 2 == 0 else 1
    groups = per_peer // each
    chips = parts // 2
    hops = max(chips - 1, 1)
    rows = max(packed_rows(depth, part) for part in range(parts))
    total_rows = sum(packed_rows(depth, part) for part in range(parts))
    vmem = pl.BlockSpec(memory_space=pltpu.VMEM)
    dma = pltpu.SemaphoreType.DMA
    at_once = 8
    outgoing, slots = pl.pallas_call(
        pack,
        in_specs=[pl.BlockSpec(memory_space=pltpu.HBM)] * 2,
        out_specs=(vmem, vmem),
        scratch_shapes=[
            pltpu.VMEM((rows + 1, at_once, lines, columns), jnp.float32),
            pltpu.SMEM((sub_count,), jnp.int32),
            pltpu.SMEM((boxes,), jnp.int32),
            pltpu.VMEM((boxes // at_once, at_once, lines * depth, columns), jnp.float32),
            dma((boxes // at_once + 1,)),
        ],
        out_shape=(
            jax.ShapeDtypeStruct((sub_count, groups, rows, each, lines, columns), jnp.float32),
            jax.ShapeDtypeStruct((sub_count, 1, LANES), jnp.int32),
        ),
        compiler_params=pltpu.CompilerParams(vmem_limit_bytes=48 * MIB),
        name="pack",
    )(
        pltpu.with_memory_space_constraint(owner_slot, pltpu.HBM),
        coefficients.reshape(boxes, lines * depth, columns),
    )

    matrix = wave_matrix(degrees, columns, K)
    high = matrix.astype(jnp.bfloat16)
    low = (matrix - high.astype(np.float32)).astype(jnp.bfloat16)
    waves, quarters, source_of = pl.pallas_call(
        exchange,
        out_shape=(
            jax.ShapeDtypeStruct((sub_count, groups, each, cases, 2 * width, K), jnp.float32),
            jax.ShapeDtypeStruct((sub_count, groups, each, cases, 2 * width, K), jnp.float32),
            jax.ShapeDtypeStruct((1, LANES), jnp.int32),
        ),
        in_specs=[vmem] * 9,
        out_specs=(vmem, vmem, vmem),
        scratch_shapes=[
            pltpu.VMEM((sub_count, 1, LANES), jnp.int32),
            pltpu.VMEM((sub_count, groups, total_rows, each, lines, columns), jnp.float32),
            pltpu.VMEM((degrees, width, lines, columns), jnp.float32),
            pltpu.VMEM((each * lines * width, columns), jnp.float32),
            dma((sub_count, groups)),
            dma((sub_count, groups)),
            dma((hops, sub_count, groups)),
            dma((hops, sub_count, groups)),
            dma((chips, sub_count, groups)),
            dma((chips, sub_count, groups)),
            dma((sub_count,)),
            dma((sub_count,)),
            dma((groups + 1,)),
            pltpu.VMEM((sub_count, groups, rows, each, lines, columns) if chips == 2 else (8, LANES), jnp.float32),
            dma((sub_count, groups)),
            dma((sub_count, groups)),
            dma((sub_count, groups)),
            dma((sub_count, groups)),
            dma((sub_count, groups)),
            dma((sub_count, groups)),
        ],
        compiler_params=pltpu.CompilerParams(
            collective_id=0, has_side_effects=True, vmem_limit_bytes=40 * MIB
        ),
        name="exchange",
    )(
        outgoing,
        slots,
        *(jnp.asarray(constant) for constant in legendre_constants(degrees, columns, parts)),
        jnp.asarray(high),
        jnp.asarray(low),
    )

    phase_cos, phase_sin = phase_tables(parts, K)
    blk = lax.axis_index("blk").astype(jnp.int32)
    count = 2 if boxes % 2 == 0 else 1
    slots = min(6, boxes // count)
    own = pl.BlockSpec((1, 8, 2 * width, K), lambda i, source, octants, part: (part[0], 0, 0, 0))
    out = pl.pallas_call(
        lambda source, octants, part, *refs: phases(source, octants, *refs),
        grid_spec=pltpu.PrefetchScalarGridSpec(
            num_scalar_prefetch=3,
            grid=(1,),
            in_specs=[vmem, vmem, own, own],
            out_specs=pl.BlockSpec(memory_space=pltpu.HBM),
            scratch_shapes=[
                pltpu.VMEM((slots, count, cases, 8, 2 * width, K), jnp.float32),
                dma((slots,)),
            ],
        ),
        out_shape=jax.ShapeDtypeStruct((boxes, cases, 8, 2 * width, K), jnp.float32),
        compiler_params=pltpu.CompilerParams(vmem_limit_bytes=32 * MIB),
        name="phases",
    )(
        source_of.reshape(-1),
        child_list.T,
        blk.reshape(1),
        waves.reshape(boxes, cases, 2 * width, K),
        quarters.reshape(boxes, cases, 2 * width, K),
        jnp.asarray(phase_cos),
        jnp.asarray(phase_sin),
    )
    return out.reshape(boxes, cases, 8, width, 2, K)


def solution(mesh):
    placed = (P("sub", None, None, "blk", None), P("sub"), P("sub", None))
    return jax.shard_map(
        body,
        mesh=mesh,
        in_specs=placed,
        out_specs=P("sub", None, None, "blk", None, None),
        check_vma=False,
    )
```
